512 devices in a mesh: tm: 128 (over x_lo, y, z), rows: 4 (over x_hi, core).
Axes of the slice: x: 4 (x_hi: 2, x_lo: 2; x = x_hi * 2 + x_lo), y: 4, z: 16, core: 2. Of those that a mesh axis runs over, the one named last changes fastest.
Arguments:
- start_state: float32 [4, 32, 512], P(None, 'rows'), may hold values from -0.15 to 1.15, as said below
- initial_guess: float32 [128, 4, 32, 512], P('tm', None, 'rows'), may hold values from -0.15 to 1.15, as said below
- land_mask: int32 [32, 512], P('rows'), may hold values 0 or 1
- bed_class: int32 [32, 512], P('rows'), may hold values from 0 to 15
- bed_table: float32 [16], replicated, may hold values from -0.5 to 0.5
Outputs:
- corrected: float32 [128, 4, 32, 512], P('tm', None, 'rows')
The draws below stay inside these ranges and needn't reach their ends.
Inputs may be any that keep to these rules, and one draw needn't show every extreme that they name: `start_state`: component 0 lies in 0.85 to 1.15, components 1 and 2 in -0.15 to 0.15, component 3 in 0.15 to 0.45. `initial_guess`: component 0 lies in 0.85 to 1.15, components 1 and 2 in -0.15 to 0.15, component 3 in 0.15 to 0.45.
All inputs are finite; a program needn't handle non-finite values. No bound on the sum of `land_mask` on one device may be relied on, other than what follows from the above.
Results may differ from the reference program's by a relative error of at most 0.00002.
Values sent between devices are 32-bit elements; how exact they have to be, the bound alone decides.
No kernel may reach another device: no remote copies, remote signals or barrier semaphores. Data moves between devices by JAX's collectives and lax.ppermute only.
A program may use at most 64 MiB of HBM per device.

```python
import jax
import jax.numpy as jnp
from jax import lax

COLUMNS = 512
FINE_STEPS = 8
BLOCK_LEN = 4
RELAXES = 2
CLASSES = 16
SLICES = 128
ALL_ROWS = 32


def make_fields(key, leading_shape):
    mesh_grid = leading_shape + (ALL_ROWS, COLUMNS)
    random_keys = jax.random.split(jax.random.fold_in(key, 17), 4)
    fluid_thickness = 1.0 + 0.05 * jnp.clip(jax.random.normal(random_keys[0], mesh_grid, jnp.float32), -3.0, 3.0)
    eastward_flux = 0.05 * jnp.clip(jax.random.normal(random_keys[1], mesh_grid, jnp.float32), -3.0, 3.0)
    northward_flux = 0.05 * jnp.clip(jax.random.normal(random_keys[2], mesh_grid, jnp.float32), -3.0, 3.0)
    suspended_load = 0.3 + 0.05 * jnp.clip(jax.random.normal(random_keys[3], mesh_grid, jnp.float32), -3.0, 3.0)
    return jnp.stack([fluid_thickness, eastward_flux, northward_flux, suspended_load], axis=len(leading_shape))


def draw_start_state(key, part):
    return make_fields(jax.random.fold_in(key, 3), ())


def draw_initial_guess(key, part):
    return make_fields(jax.random.fold_in(key, 5), (SLICES,))


def with_ends(entries, stream_key, smallest, top_value):
    extent = entries.shape
    index_at = [jax.random.randint(jax.random.fold_in(stream_key, axis), (), 0, extent[axis]) for axis in range(len(extent))]
    entries = entries.at[tuple(index_at)].set(smallest)
    longest = extent.index(max(extent))
    index_at[longest] = (index_at[longest] + 1) % extent[longest]
    return entries.at[tuple(index_at)].set(top_value)


def setup_inputs(seed: int = 0) -> dict:
    keys = jax.random.split(jax.random.key(seed), 6)
    return {
        "start_state": draw_start_state(jax.random.fold_in(keys[5], 71), 0),
        "initial_guess": draw_initial_guess(jax.random.fold_in(keys[5], 71), 0),
        "land_mask": with_ends((jax.random.randint(keys[2], (ALL_ROWS, COLUMNS), 0, 8) < 7).astype(jnp.int32), jax.random.fold_in(keys[2], 1), 0, 1),
        "bed_class": with_ends(jax.random.randint(keys[3], (ALL_ROWS, COLUMNS), 0, CLASSES), jax.random.fold_in(keys[3], 1), 0, CLASSES - 1).astype(jnp.int32),
        "bed_table": jnp.clip(jax.random.uniform(keys[4], (CLASSES,), jnp.float32, -0.5, 0.5), -0.5, 0.5),
    }


def across(values, array_axis):
    return jnp.roll(values, -1, axis=array_axis) - jnp.roll(values, 1, axis=array_axis)

def advance(model_state, bed_level, wet_cells, stability_ratio, viscous):
    fluid_thickness = model_state[0]
    eastward_flux = model_state[1]
    northward_flux = model_state[2]
    suspended_load = model_state[3]
    east_velocity = eastward_flux / fluid_thickness
    north_velocity = northward_flux / fluid_thickness
    pressure_term = 0.5 * fluid_thickness * fluid_thickness
    column_fluxes = jnp.stack([eastward_flux, eastward_flux * east_velocity + pressure_term, northward_flux * east_velocity, suspended_load * east_velocity])
    row_fluxes = jnp.stack([northward_flux, eastward_flux * north_velocity, northward_flux * north_velocity + pressure_term, suspended_load * north_velocity])
    neighbours = jnp.roll(model_state, -1, axis=-1) + jnp.roll(model_state, 1, axis=-1) + jnp.roll(model_state, -1, axis=-2) + jnp.roll(model_state, 1, axis=-2)
    advanced_fields = model_state - 0.5 * stability_ratio * (across(column_fluxes, -1) + across(row_fluxes, -2)) + viscous * (neighbours - 4.0 * model_state)
    flow_magnitude = jnp.sqrt(east_velocity * east_velocity + north_velocity * north_velocity)
    slope_east = 0.5 * across(bed_level, -1)
    slope_north = 0.5 * across(bed_level, -2)
    new_zonal_motion = wet_cells * (advanced_fields[1] - stability_ratio * (fluid_thickness * slope_east + 0.02 * flow_magnitude * east_velocity))
    new_meridional_motion = wet_cells * (advanced_fields[2] - stability_ratio * (fluid_thickness * slope_north + 0.02 * flow_magnitude * north_velocity))
    new_bedload_amount = advanced_fields[3] + stability_ratio * (0.05 * flow_magnitude * flow_magnitude - 0.3 * suspended_load / fluid_thickness)
    return jnp.stack([advanced_fields[0], new_zonal_motion, new_meridional_motion, new_bedload_amount])

def reference(start_state, initial_guess, land_mask, bed_class, bed_table):
    bed_level = bed_table[bed_class]
    wet_cells = land_mask.astype(jnp.float32)

    def fine_path(model_state):
        for repeat in range(FINE_STEPS):
            model_state = advance(model_state, bed_level, wet_cells, 0.0375, 0.025)
        return model_state

    def coarse_step(model_state):
        return advance(model_state, bed_level, wet_cells, 0.3, 0.2)

    def both_paths(model_state):
        return fine_path(model_state) - coarse_step(model_state)
    openings = jnp.concatenate([start_state[None], initial_guess[:-1]], axis=0)
    updated = lax.map(fine_path, openings)
    befores = jnp.concatenate([start_state[None], updated[:-1]], axis=0)
    forcing = lax.map(both_paths, befores)
    blocks = SLICES // BLOCK_LEN
    forcing_blocks = forcing.reshape((blocks, BLOCK_LEN) + forcing.shape[1:])
    values = updated.reshape((blocks, BLOCK_LEN) + forcing.shape[1:])

    def sweep_block(paired):
        opening, block_forcing = paired
        block_values = []
        for offset in range(BLOCK_LEN):
            opening = coarse_step(opening) + block_forcing[offset]
            block_values.append(opening)
        return jnp.stack(block_values)
    for relax_turn in range(RELAXES):
        endings = values[:, BLOCK_LEN - 1]
        block_openings = jnp.concatenate([start_state[None], endings[:-1]], axis=0)
        values = lax.map(sweep_block, (block_openings, forcing_blocks))
    return values.reshape(forcing.shape)
```

```python
import jax
import jax.numpy as jnp
from jax import lax
from jax.experimental import pallas as pl
from jax.experimental.pallas import tpu as pltpu
from jax.sharding import PartitionSpec as P

FINE_STEPS = 8
FINE = (0.0375, 0.025)
COARSE = (0.3, 0.2)
FIELDS = 4
TILE = (8, 128)
AXES = ("tm", "rows")


def east(x):
    return pltpu.roll(x, 127, 1)


def west(x):
    return pltpu.roll(x, 1, 1)


def north(tiles):
    return [*tiles[1:], pltpu.roll(tiles[0], 7, 0)]


def south(tiles):
    return [pltpu.roll(tiles[3], 1, 0), *tiles[:3]]


def advance(state, statics, ratio, viscous):
    slope_e, slope_n, wet = statics
    half = 0.5 * ratio
    h, p, s, m = state
    inverse = [1.0 / a for a in h]
    u = [a * b for a, b in zip(p, inverse)]
    v = [a * b for a, b in zip(s, inverse)]
    hu = [half * a for a in u]
    hv = [half * a for a in v]
    pressure = [(0.5 * half) * (a * a) for a in h]
    cross = [a * b for a, b in zip(s, hu)]
    east_flux = (
        [half * a for a in p],
        [a * b + c for a, b, c in zip(p, hu, pressure)],
        cross,
        [a * b for a, b in zip(m, hu)],
    )
    north_flux = (
        [half * a for a in s],
        cross,
        [a * b + c for a, b, c in zip(s, hv, pressure)],
        [a * b for a, b in zip(m, hv)],
    )
    moved = []
    for field in range(FIELDS):
        q = state[field]
        near = [viscous * a for a in q]
        up = north([a - b for a, b in zip(near, north_flux[field])])
        down = south([a + b for a, b in zip(near, north_flux[field])])
        tiles = []
        for k in range(4):
            lanes = east(near[k] - east_flux[field][k]) + west(near[k] + east_flux[field][k])
            tiles.append((1.0 - 4.0 * viscous) * q[k] + (lanes + (up[k] + down[k])))
        moved.append(tiles)
    new_p, new_s, new_m = [], [], []
    for k in range(4):
        square = u[k] * u[k] + v[k] * v[k]
        drag = (0.02 * ratio) * jnp.sqrt(square)
        new_p.append(wet[k] * (moved[1][k] - (h[k] * slope_e[k] + drag * u[k])))
        new_s.append(wet[k] * (moved[2][k] - (h[k] * slope_n[k] + drag * v[k])))
        new_m.append(
            moved[3][k] + ((0.05 * ratio) * square - (0.3 * ratio) * (m[k] * inverse[k]))
        )
    return [moved[0], new_p, new_s, new_m]


def scaled(slopes, ratio):
    slope_e, slope_n, wet = slopes
    return [ratio * a for a in slope_e], [ratio * a for a in slope_n], wet


def flat(nested):
    return jax.tree.leaves(nested)


def combine(function, a, b):
    return jax.tree.map(function, a, b)


def read_tiles(ref, *lead):
    return [[ref[(*lead, field, k)] for k in range(4)] for field in range(FIELDS)]


def write_tiles(ref, state, *lead):
    for field in range(FIELDS):
        for k in range(4):
            ref[(*lead, field, k)] = state[field][k]


def lane_index():
    return lax.broadcasted_iota(jnp.int32, TILE, 1)


def pack_kernel(start_ref, guess_ref, mask_ref, class_ref, table_ref, out_ref):
    time_index = lax.axis_index("tm")
    lanes = lane_index()
    use_start = time_index >= lax.axis_size("tm") - 2
    odd = time_index % 2 == 1

    def windows(plane, chunks):
        ahead = [pltpu.roll(a, 32, 1) for a in chunks]
        behind = [pltpu.roll(a, 96, 1) for a in chunks]
        for c in range(4):
            out_ref[2 * c, plane] = jnp.where(lanes < 32, ahead[c - 1], ahead[c])
            out_ref[2 * c + 1, plane] = jnp.where(lanes < 96, behind[c], behind[(c + 1) % 4])

    cuts = [pl.ds(128 * c, 128) for c in range(4)]
    for field in range(FIELDS):
        windows(
            field,
            [jnp.where(use_start, start_ref[field, :, cut], guess_ref[0, field, :, cut]) for cut in cuts],
        )
    static = []
    for cut in cuts:
        classes = class_ref[:, cut]
        bed = jnp.zeros(TILE, jnp.float32)
        for index in range(table_ref.shape[0]):
            bed = jnp.where(classes == index, table_ref[index], bed)
        static.append(jnp.where(odd, mask_ref[:, cut].astype(jnp.float32), bed))
    windows(FIELDS, static)


def forcing_kernel(in_ref, forcing_ref, chain_ref, before_ref, slope_ref, rows_ref):
    group = lax.axis_index("tm") // 2
    last = group == lax.axis_size("tm") // 2 - 1
    for pair in range(2):
        for r in range(4):
            for plane in range(FIELDS + 1):
                rows_ref[pair, plane, pl.ds(8 * r, 8), :] = in_ref[4 * pair + r, plane]

    def strided(pair, plane):
        return [rows_ref[pair, plane, pl.ds(k, 8, 4), :] for k in range(4)]

    bed, wet = strided(0, FIELDS), strided(1, FIELDS)
    slope_e = [0.5 * (east(a) - west(a)) for a in bed]
    slope_n = [0.5 * (a - b) for a, b in zip(north(bed), south(bed))]
    slopes = (slope_e, slope_n, wet)
    for index, tiles in enumerate(slopes):
        for k in range(4):
            slope_ref[index, k] = tiles[k]
    fine, coarse = scaled(slopes, FINE[0]), scaled(slopes, COARSE[0])
    first = [[strided(pair, field) for field in range(FIELDS)] for pair in range(2)]
    shape = jax.tree.structure(first)

    def propagate(states):
        def body(_, leaves):
            pairs = jax.tree.unflatten(shape, leaves)
            return tuple(flat([advance(state, fine, *FINE) for state in pairs]))

        return jax.tree.unflatten(shape, lax.fori_loop(0, FINE_STEPS, body, tuple(flat(states))))

    before = propagate(first)
    before[0] = combine(lambda a, b: jnp.where(last, a, b), first[0], before[0])
    write_tiles(before_ref, before[0])
    reached = propagate(before)
    forcing = [
        combine(jnp.subtract, reached[pair], advance(before[pair], coarse, *COARSE))
        for pair in range(2)
    ]
    for pair in range(2):
        write_tiles(forcing_ref, forcing[pair], pair)
    write_tiles(chain_ref, combine(jnp.add, advance(reached[0], coarse, *COARSE), forcing[1]))


def two_steps(opening, forcing_ref, slope_ref):
    slopes = [[slope_ref[index, k] for k in range(4)] for index in range(3)]
    coarse = scaled(slopes, COARSE[0])
    values = []
    for pair in range(2):
        opening = combine(
            jnp.add, advance(opening, coarse, *COARSE), read_tiles(forcing_ref, pair)
        )
        values.append(opening)
    return values


def first_chain_kernel(in_ref, forcing_ref, slope_ref, out_ref):
    write_tiles(out_ref, two_steps(read_tiles(in_ref), forcing_ref, slope_ref)[1])


def second_chain_kernel(in_ref, before_ref, forcing_ref, slope_ref, out_ref):
    group = lax.axis_index("tm") // 2
    last = group == lax.axis_size("tm") // 2 - 1
    opening = combine(lambda a, b: jnp.where(last, a, b), read_tiles(before_ref), read_tiles(in_ref))
    for pair, value in enumerate(two_steps(opening, forcing_ref, slope_ref)):
        write_tiles(out_ref, value, pair)


def last_chain_kernel(in_ref, forcing_ref, slope_ref, out_ref, rows_ref):
    lanes = lane_index()
    states = [read_tiles(in_ref, 0), read_tiles(in_ref, 1)]
    states += two_steps(states[1], forcing_ref, slope_ref)
    for position in range(4):
        for field in range(FIELDS):
            shift = 96 if field % 2 == 0 else 32
            for k in range(4):
                rows_ref[position, field, pl.ds(k, 8, 4), :] = pltpu.roll(
                    states[position][field][k], shift, 1
                )
        for r in range(4):
            for half in range(2):
                low = rows_ref[position, 2 * half, pl.ds(8 * r, 8), :]
                high = rows_ref[position, 2 * half + 1, pl.ds(8 * r, 8), :]
                out_ref[4 * position + r, half] = jnp.where(lanes < 64, low, high)


def unpack_kernel(in_ref, out_ref):
    lanes = lane_index()
    for half in range(2):
        for c in range(4):
            left, right = in_ref[2 * c, half], in_ref[2 * c + 1, half]
            cut = pl.ds(128 * c, 128)
            out_ref[0, 2 * half, :, cut] = jnp.where(lanes < 64, left, pltpu.roll(right, 64, 1))
            out_ref[0, 2 * half + 1, :, cut] = jnp.where(lanes < 64, pltpu.roll(left, 64, 1), right)


def call(kernel, shapes, name, specs=None, scratch=()):
    outs = [jax.ShapeDtypeStruct(shape, jnp.float32) for shape in shapes]
    vmem = pl.BlockSpec(memory_space=pltpu.VMEM)
    single = len(outs) == 1

    def run(*args):
        return pl.pallas_call(
            kernel,
            out_shape=outs[0] if single else outs,
            in_specs=specs or [vmem] * len(args),
            out_specs=vmem if single else [vmem] * len(outs),
            scratch_shapes=scratch,
            name=name,
        )(*args)

    return run


def groups(count, row_devices, size):
    return [
        [(size * g + q) * row_devices + r for q in range(size) for r in range(row_devices)]
        for g in range(count // size)
    ]


def on_device(start_state, initial_guess, land_mask, bed_class, bed_table):
    count, row_devices = lax.axis_size("tm"), lax.axis_size("rows")
    vmem = pl.BlockSpec(memory_space=pltpu.VMEM)
    smem = pl.BlockSpec(memory_space=pltpu.SMEM)
    packed = call(
        pack_kernel, [(8, FIELDS + 1, *TILE)], "pack", [vmem] * 4 + [smem]
    )(start_state, initial_guess, land_mask, bed_class, bed_table)
    arrived = lax.all_to_all(packed, AXES, 0, 0, axis_index_groups=groups(count, row_devices, 2))
    state = (FIELDS, 4, *TILE)
    forcing, chain, before, slopes = call(
        forcing_kernel,
        [(2, *state), state, state, (3, 4, *TILE)],
        "forcing",
        scratch=[pltpu.VMEM((2, FIELDS + 1, 32, 128), jnp.float32)],
    )(arrived)
    to_even = [(i, (i + 2) % count) for i in range(count) if i % 4 >= 2]
    to_odd = [(i, i + 2) for i in range(count) if i % 4 < 2]
    chain = lax.ppermute(chain, "tm", to_even)
    chain = call(first_chain_kernel, [state], "chain1")(chain, forcing, slopes)
    chain = lax.ppermute(chain, "tm", to_odd)
    values = call(second_chain_kernel, [(2, *state)], "chain2")(chain, before, forcing, slopes)
    values = lax.ppermute(values, "tm", to_even)
    packed = call(
        last_chain_kernel,
        [(16, 2, *TILE)],
        "chain3",
        scratch=[pltpu.VMEM((4, FIELDS, 32, 128), jnp.float32)],
    )(values, forcing, slopes)
    arrived = lax.all_to_all(packed, AXES, 0, 0, axis_index_groups=groups(count, row_devices, 4))
    return call(unpack_kernel, [initial_guess.shape], "unpack")(arrived)


def solution(mesh):
    in_specs = (
        P(None, "rows", None),
        P("tm", None, "rows", None),
        P("rows", None),
        P("rows", None),
        P(),
    )
    out_specs = P("tm", None, "rows", None)
    return jax.shard_map(
        on_device, mesh=mesh, in_specs=in_specs, out_specs=out_specs, check_vma=False
    )
```

```python
import jax
import jax.numpy as jnp
from jax import lax
from jax.experimental import pallas as pl
from jax.experimental.pallas import tpu as pltpu
from jax.sharding import PartitionSpec as P

FINE_STEPS = 8
FINE = (0.0375, 0.025)
COARSE = (0.3, 0.2)
FIELDS = 4
TILE = (8, 128)
AXES = ("tm", "rows")


def east(x):
    return pltpu.roll(x, 127, 1)


def west(x):
    return pltpu.roll(x, 1, 1)


def north(tiles):
    return [*tiles[1:], pltpu.roll(tiles[0], 7, 0)]


def south(tiles):
    return [pltpu.roll(tiles[3], 1, 0), *tiles[:3]]


def advance(state, statics, ratio, viscous):
    slope_e, slope_n, wet = statics
    half = 0.5 * ratio
    h, p, s, m = state
    inverse = [1.0 / a for a in h]
    u = [a * b for a, b in zip(p, inverse)]
    v = [a * b for a, b in zip(s, inverse)]
    hu = [half * a for a in u]
    hv = [half * a for a in v]
    pressure = [(0.5 * half) * (a * a) for a in h]
    cross = [a * b for a, b in zip(s, hu)]
    east_flux = (
        [half * a for a in p],
        [a * b + c for a, b, c in zip(p, hu, pressure)],
        cross,
        [a * b for a, b in zip(m, hu)],
    )
    north_flux = (
        [half * a for a in s],
        cross,
        [a * b + c for a, b, c in zip(s, hv, pressure)],
        [a * b for a, b in zip(m, hv)],
    )
    moved = []
    for field in range(FIELDS):
        q = state[field]
        near = [viscous * a for a in q]
        up = north([a - b for a, b in zip(near, north_flux[field])])
        down = south([a + b for a, b in zip(near, north_flux[field])])
        tiles = []
        for k in range(4):
            lanes = east(near[k] - east_flux[field][k]) + west(near[k] + east_flux[field][k])
            tiles.append((1.0 - 4.0 * viscous) * q[k] + (lanes + (up[k] + down[k])))
        moved.append(tiles)
    new_p, new_s, new_m = [], [], []
    for k in range(4):
        square = u[k] * u[k] + v[k] * v[k]
        drag = (0.02 * ratio) * jnp.sqrt(square)
        new_p.append(wet[k] * (moved[1][k] - (h[k] * slope_e[k] + drag * u[k])))
        new_s.append(wet[k] * (moved[2][k] - (h[k] * slope_n[k] + drag * v[k])))
        new_m.append(
            moved[3][k] + ((0.05 * ratio) * square - (0.3 * ratio) * (m[k] * inverse[k]))
        )
    return [moved[0], new_p, new_s, new_m]


def scaled(slopes, ratio):
    slope_e, slope_n, wet = slopes
    return [ratio * a for a in slope_e], [ratio * a for a in slope_n], wet


def flat(nested):
    return jax.tree.leaves(nested)


def combine(function, a, b):
    return jax.tree.map(function, a, b)


def read_tiles(ref, *lead):
    return [[ref[(*lead, field, k)] for k in range(4)] for field in range(FIELDS)]


def write_tiles(ref, state, *lead):
    for field in range(FIELDS):
        for k in range(4):
            ref[(*lead, field, k)] = state[field][k]


def lane_index():
    return lax.broadcasted_iota(jnp.int32, TILE, 1)


def pack_kernel(start_ref, guess_ref, mask_ref, class_ref, table_ref, out_ref):
    time_index = lax.axis_index("tm")
    lanes = lane_index()
    use_start = time_index >= lax.axis_size("tm") - 2
    odd = time_index % 2 == 1

    def windows(plane, chunks):
        ahead = [pltpu.roll(a, 32, 1) for a in chunks]
        behind = [pltpu.roll(a, 96, 1) for a in chunks]
        for c in range(4):
            out_ref[2 * c, plane] = jnp.where(lanes < 32, ahead[c - 1], ahead[c])
            out_ref[2 * c + 1, plane] = jnp.where(lanes < 96, behind[c], behind[(c + 1) % 4])

    cuts = [pl.ds(128 * c, 128) for c in range(4)]
    for field in range(FIELDS):
        windows(
            field,
            [jnp.where(use_start, start_ref[field, :, cut], guess_ref[0, field, :, cut]) for cut in cuts],
        )
    static = []
    for cut in cuts:
        classes = class_ref[:, cut]
        bed = jnp.zeros(TILE, jnp.float32)
        for index in range(table_ref.shape[0]):
            bed = jnp.where(classes == index, table_ref[index], bed)
        static.append(jnp.where(odd, mask_ref[:, cut].astype(jnp.float32), bed))
    windows(FIELDS, static)


def forcing_kernel(in_ref, forcing_ref, chain_ref, before_ref, slope_ref, rows_ref):
    group = lax.axis_index("tm") // 2
    last = group == lax.axis_size("tm") // 2 - 1
    for pair in range(2):
        for r in range(4):
            for plane in range(FIELDS + 1):
                rows_ref[pair, plane, pl.ds(8 * r, 8), :] = in_ref[4 * pair + r, plane]

    def strided(pair, plane):
        return [rows_ref[pair, plane, pl.ds(k, 8, 4), :] for k in range(4)]

    bed, wet = strided(0, FIELDS), strided(1, FIELDS)
    slope_e = [0.5 * (east(a) - west(a)) for a in bed]
    slope_n = [0.5 * (a - b) for a, b in zip(north(bed), south(bed))]
    slopes = (slope_e, slope_n, wet)
    for index, tiles in enumerate(slopes):
        for k in range(4):
            slope_ref[index, k] = tiles[k]
    fine, coarse = scaled(slopes, FINE[0]), scaled(slopes, COARSE[0])
    first = [[strided(pair, field) for field in range(FIELDS)] for pair in range(2)]
    shape = jax.tree.structure(first)

    def propagate(states):
        def body(_, leaves):
            pairs = jax.tree.unflatten(shape, leaves)
            return tuple(flat([advance(state, fine, *FINE) for state in pairs]))

        return jax.tree.unflatten(shape, lax.fori_loop(0, FINE_STEPS, body, tuple(flat(states))))

    before = propagate(first)
    before[0] = combine(lambda a, b: jnp.where(last, a, b), first[0], before[0])
    write_tiles(before_ref, before[0])
    reached = propagate(before)
    forcing = [
        combine(jnp.subtract, reached[pair], advance(before[pair], coarse, *COARSE))
        for pair in range(2)
    ]
    for pair in range(2):
        write_tiles(forcing_ref, forcing[pair], pair)
    write_tiles(chain_ref, combine(jnp.add, advance(reached[0], coarse, *COARSE), forcing[1]))


def two_steps(opening, forcing_ref, slope_ref):
    slopes = [[slope_ref[index, k] for k in range(4)] for index in range(3)]
    coarse = scaled(slopes, COARSE[0])
    values = []
    for pair in range(2):
        opening = combine(
            jnp.add, advance(opening, coarse, *COARSE), read_tiles(forcing_ref, pair)
        )
        values.append(opening)
    return values


def first_chain_kernel(in_ref, forcing_ref, slope_ref, out_ref):
    write_tiles(out_ref, two_steps(read_tiles(in_ref), forcing_ref, slope_ref)[1])


def second_chain_kernel(in_ref, before_ref, forcing_ref, slope_ref, out_ref):
    group = lax.axis_index("tm") // 2
    last = group == lax.axis_size("tm") // 2 - 1
    opening = combine(lambda a, b: jnp.where(last, a, b), read_tiles(before_ref), read_tiles(in_ref))
    for pair, value in enumerate(two_steps(opening, forcing_ref, slope_ref)):
        write_tiles(out_ref, value, pair)


def last_chain_kernel(in_ref, forcing_ref, slope_ref, out_ref, rows_ref):
    lanes = lane_index()
    states = [read_tiles(in_ref, 0), read_tiles(in_ref, 1)]
    states += two_steps(states[1], forcing_ref, slope_ref)
    for position in range(4):
        for field in range(FIELDS):
            shift = 96 if field % 2 == 0 else 32
            for k in range(4):
                rows_ref[position, field, pl.ds(k, 8, 4), :] = pltpu.roll(
                    states[position][field][k], shift, 1
                )
        for r in range(4):
            for half in range(2):
                low = rows_ref[position, 2 * half, pl.ds(8 * r, 8), :]
                high = rows_ref[position, 2 * half + 1, pl.ds(8 * r, 8), :]
                out_ref[4 * position + r, half] = jnp.where(lanes < 64, low, high)


def unpack_kernel(in_ref, out_ref):
    lanes = lane_index()
    for half in range(2):
        for c in range(4):
            left, right = in_ref[2 * c, half], in_ref[2 * c + 1, half]
            cut = pl.ds(128 * c, 128)
            out_ref[0, 2 * half, :, cut] = jnp.where(lanes < 64, left, pltpu.roll(right, 64, 1))
            out_ref[0, 2 * half + 1, :, cut] = jnp.where(lanes < 64, pltpu.roll(left, 64, 1), right)


def call(kernel, shapes, name, specs=None, scratch=(), in_vmem=True, out_vmem=True):
    kind = pltpu.VMEM if out_vmem else jax.ShapeDtypeStruct
    outs = [kind(shape, jnp.float32) for shape in shapes]
    vmem = pl.BlockSpec(memory_space=pltpu.VMEM)
    single = len(outs) == 1

    def run(*args):
        if in_vmem:
            args = [pltpu.with_memory_space_constraint(a, pltpu.VMEM) for a in args]
        return pl.pallas_call(
            kernel,
            out_shape=outs[0] if single else outs,
            in_specs=specs or [vmem] * len(args),
            out_specs=vmem if single else [vmem] * len(outs),
            scratch_shapes=scratch,
            name=name,
        )(*args)

    return run


def groups(count, row_devices, size):
    return [
        [(size * g + q) * row_devices + r for q in range(size) for r in range(row_devices)]
        for g in range(count // size)
    ]


def on_device(start_state, initial_guess, land_mask, bed_class, bed_table):
    count, row_devices = lax.axis_size("tm"), lax.axis_size("rows")
    vmem = pl.BlockSpec(memory_space=pltpu.VMEM)
    smem = pl.BlockSpec(memory_space=pltpu.SMEM)
    packed = call(
        pack_kernel, [(8, FIELDS + 1, *TILE)], "pack", [vmem] * 4 + [smem], in_vmem=False
    )(start_state, initial_guess, land_mask, bed_class, bed_table)
    arrived = lax.all_to_all(packed, AXES, 0, 0, axis_index_groups=groups(count, row_devices, 2))
    state = (FIELDS, 4, *TILE)
    forcing, chain, before, slopes = call(
        forcing_kernel,
        [(2, *state), state, state, (3, 4, *TILE)],
        "forcing",
        scratch=[pltpu.VMEM((2, FIELDS + 1, 32, 128), jnp.float32)],
    )(arrived)
    to_even = [(i, (i + 2) % count) for i in range(count) if i % 4 >= 2]
    to_odd = [(i, i + 2) for i in range(count) if i % 4 < 2]
    chain = lax.ppermute(chain, "tm", to_even)
    chain = call(first_chain_kernel, [state], "chain1")(chain, forcing, slopes)
    chain = lax.ppermute(chain, "tm", to_odd)
    values = call(second_chain_kernel, [(2, *state)], "chain2")(chain, before, forcing, slopes)
    values = lax.ppermute(values, "tm", to_even)
    packed = call(
        last_chain_kernel,
        [(16, 2, *TILE)],
        "chain3",
        scratch=[pltpu.VMEM((4, FIELDS, 32, 128), jnp.float32)],
    )(values, forcing, slopes)
    arrived = lax.all_to_all(packed, AXES, 0, 0, axis_index_groups=groups(count, row_devices, 4))
    return call(unpack_kernel, [initial_guess.shape], "unpack", out_vmem=False)(arrived)


def solution(mesh):
    in_specs = (
        P(None, "rows", None),
        P("tm", None, "rows", None),
        P("rows", None),
        P("rows", None),
        P(),
    )
    out_specs = P("tm", None, "rows", None)
    return jax.shard_map(
        on_device, mesh=mesh, in_specs=in_specs, out_specs=out_specs, check_vma=False
    )
```

```python
import jax
import jax.numpy as jnp
from jax import lax
from jax.experimental import pallas as pl
from jax.experimental.pallas import tpu as pltpu
from jax.sharding import PartitionSpec as P

FINE_STEPS = 8
FINE = (0.0375, 0.025)
COARSE = (0.3, 0.2)
FIELDS = 4
TILE = (8, 128)
AXES = ("tm", "rows")


def east(x):
    return pltpu.roll(x, 127, 1)


def west(x):
    return pltpu.roll(x, 1, 1)


def north(tiles):
    return [*tiles[1:], pltpu.roll(tiles[0], 7, 0)]


def south(tiles):
    return [pltpu.roll(tiles[3], 1, 0), *tiles[:3]]


def advance(state, statics, ratio, viscous):
    slope_e, slope_n, wet = statics
    half = 0.5 * ratio
    h, p, s, m = state
    inverse = [1.0 / a for a in h]
    u = [a * b for a, b in zip(p, inverse)]
    v = [a * b for a, b in zip(s, inverse)]
    hu = [half * a for a in u]
    hv = [half * a for a in v]
    pressure = [(0.5 * half) * (a * a) for a in h]
    cross = [a * b for a, b in zip(s, hu)]
    east_flux = (
        [half * a for a in p],
        [a * b + c for a, b, c in zip(p, hu, pressure)],
        cross,
        [a * b for a, b in zip(m, hu)],
    )
    north_flux = (
        [half * a for a in s],
        cross,
        [a * b + c for a, b, c in zip(s, hv, pressure)],
        [a * b for a, b in zip(m, hv)],
    )
    moved = []
    for field in range(FIELDS):
        q = state[field]
        near = [viscous * a for a in q]
        up = north([a - b for a, b in zip(near, north_flux[field])])
        down = south([a + b for a, b in zip(near, north_flux[field])])
        tiles = []
        for k in range(4):
            lanes = east(near[k] - east_flux[field][k]) + west(near[k] + east_flux[field][k])
            tiles.append((1.0 - 4.0 * viscous) * q[k] + (lanes + (up[k] + down[k])))
        moved.append(tiles)
    new_p, new_s, new_m = [], [], []
    for k in range(4):
        square = u[k] * u[k] + v[k] * v[k]
        drag = (0.02 * ratio) * jnp.sqrt(square)
        new_p.append(wet[k] * (moved[1][k] - (h[k] * slope_e[k] + drag * u[k])))
        new_s.append(wet[k] * (moved[2][k] - (h[k] * slope_n[k] + drag * v[k])))
        new_m.append(
            moved[3][k] + ((0.05 * ratio) * square - (0.3 * ratio) * (m[k] * inverse[k]))
        )
    return [moved[0], new_p, new_s, new_m]


def scaled(slopes, ratio):
    slope_e, slope_n, wet = slopes
    return [ratio * a for a in slope_e], [ratio * a for a in slope_n], wet


def flat(nested):
    return jax.tree.leaves(nested)


def combine(function, a, b):
    return jax.tree.map(function, a, b)


def read_tiles(ref, *lead):
    return [[ref[(*lead, field, k)] for k in range(4)] for field in range(FIELDS)]


def write_tiles(ref, state, *lead):
    for field in range(FIELDS):
        for k in range(4):
            ref[(*lead, field, k)] = state[field][k]


def lane_index():
    return lax.broadcasted_iota(jnp.int32, TILE, 1)


def pack_kernel(start_ref, guess_ref, mask_ref, class_ref, table_ref, out_ref):
    time_index = lax.axis_index("tm")
    lanes = lane_index()
    use_start = time_index >= lax.axis_size("tm") - 2
    odd = time_index % 2 == 1

    def windows(plane, chunks):
        ahead = [pltpu.roll(a, 32, 1) for a in chunks]
        behind = [pltpu.roll(a, 96, 1) for a in chunks]
        for c in range(4):
            out_ref[2 * c, plane] = jnp.where(lanes < 32, ahead[c - 1], ahead[c])
            out_ref[2 * c + 1, plane] = jnp.where(lanes < 96, behind[c], behind[(c + 1) % 4])

    cuts = [pl.ds(128 * c, 128) for c in range(4)]
    for field in range(FIELDS):
        windows(
            field,
            [jnp.where(use_start, start_ref[field, :, cut], guess_ref[0, field, :, cut]) for cut in cuts],
        )
    static = []
    for cut in cuts:
        classes = class_ref[:, cut]
        bed = jnp.zeros(TILE, jnp.float32)
        for index in range(table_ref.shape[0]):
            bed = jnp.where(classes == index, table_ref[index], bed)
        static.append(jnp.where(odd, mask_ref[:, cut].astype(jnp.float32), bed))
    windows(FIELDS, static)


def fold(ref, state, *lead):
    lanes = lane_index()
    for half in range(2):
        for k in range(4):
            low = pltpu.roll(state[2 * half][k], 96, 1)
            high = pltpu.roll(state[2 * half + 1][k], 32, 1)
            ref[(*lead, 4 * half + k)] = jnp.where(lanes < 64, low, high)
        edge = None
        for slot in range(8):
            tile = state[2 * half + slot // 4][slot % 4]
            left = pltpu.roll(tile, (16 * slot - 24) % 128, 1)
            right = pltpu.roll(tile, (16 * slot + 8 - 96) % 128, 1)
            both = jnp.where(lanes < 16 * slot + 8, left, right)
            edge = both if edge is None else jnp.where(lanes < 16 * slot, edge, both)
        ref[(*lead, 8 + half)] = edge


def unfold(ref, *lead):
    lanes = lane_index()
    state = [[None] * 4 for _ in range(FIELDS)]
    for half in range(2):
        edge = ref[(*lead, 8 + half)]
        for slot in range(8):
            k = slot % 4
            own = pltpu.roll(ref[(*lead, 4 * half + k)], 32 if slot < 4 else 96, 1)
            left = pltpu.roll(edge, (24 - 16 * slot) % 128, 1)
            right = pltpu.roll(edge, (96 - 16 * slot - 8) % 128, 1)
            state[2 * half + slot // 4][k] = jnp.where(
                lanes < 32, left, jnp.where(lanes < 96, own, right)
            )
    return state


def forcing_kernel(in_ref, forcing_ref, chain_ref, pass_ref, slope_ref, rows_ref):
    group = lax.axis_index("tm") // 2
    last = group == lax.axis_size("tm") // 2 - 1
    for pair in range(2):
        for r in range(4):
            for plane in range(FIELDS + 1):
                rows_ref[pair, plane, pl.ds(8 * r, 8), :] = in_ref[4 * pair + r, plane]

    def strided(pair, plane):
        return [rows_ref[pair, plane, pl.ds(k, 8, 4), :] for k in range(4)]

    bed, wet = strided(0, FIELDS), strided(1, FIELDS)
    slope_e = [0.5 * (east(a) - west(a)) for a in bed]
    slope_n = [0.5 * (a - b) for a, b in zip(north(bed), south(bed))]
    slopes = (slope_e, slope_n, wet)
    for index, tiles in enumerate(slopes):
        for k in range(4):
            slope_ref[index, k] = tiles[k]
    fine, coarse = scaled(slopes, FINE[0]), scaled(slopes, COARSE[0])
    first = [[strided(pair, field) for field in range(FIELDS)] for pair in range(2)]
    shape = jax.tree.structure(first)

    def propagate(states):
        def body(_, leaves):
            pairs = jax.tree.unflatten(shape, leaves)
            return tuple(flat([advance(state, fine, *FINE) for state in pairs]))

        return jax.tree.unflatten(shape, lax.fori_loop(0, FINE_STEPS, body, tuple(flat(states))))

    def choose(a, b):
        return combine(lambda x, y: jnp.where(last, x, y), a, b)

    before = propagate(first)
    before[0] = choose(first[0], before[0])
    reached = propagate(before)
    forcing = [
        combine(jnp.subtract, reached[pair], advance(before[pair], coarse, *COARSE))
        for pair in range(2)
    ]
    second = combine(jnp.add, advance(reached[0], coarse, *COARSE), forcing[1])
    fold(chain_ref, second)
    fold(pass_ref, choose(reached[0], forcing[0]), 0)
    fold(pass_ref, choose(second, forcing[1]), 1)
    for pair in range(2):
        write_tiles(forcing_ref, forcing[pair], pair)


def coarse_of(slope_ref):
    return scaled([[slope_ref[index, k] for k in range(4)] for index in range(3)], COARSE[0])


def relax(opening, forcing, coarse):
    return combine(jnp.add, advance(opening, coarse, *COARSE), forcing)


def chain_kernel(in_ref, forcing_ref, slope_ref, out_ref):
    coarse = coarse_of(slope_ref)
    value = unfold(in_ref)
    for pair in range(2):
        value = relax(value, read_tiles(forcing_ref, pair), coarse)
    fold(out_ref, value)


def last_kernel(in_ref, pass_ref, forcing_ref, slope_ref, out_ref, rows_ref):
    lanes = lane_index()
    opens = lax.axis_index("tm") < 2
    coarse = coarse_of(slope_ref)
    value = unfold(in_ref)
    for position in range(4):
        if position < 2:
            given = unfold(pass_ref, position)
            value = combine(
                lambda a, b: jnp.where(opens, a, b), given, relax(value, given, coarse)
            )
        else:
            value = relax(value, read_tiles(forcing_ref, position - 2), coarse)
        for field in range(FIELDS):
            shift = 96 if field % 2 == 0 else 32
            for k in range(4):
                rows_ref[position, field, pl.ds(k, 8, 4), :] = pltpu.roll(value[field][k], shift, 1)
        for r in range(4):
            for half in range(2):
                low = rows_ref[position, 2 * half, pl.ds(8 * r, 8), :]
                high = rows_ref[position, 2 * half + 1, pl.ds(8 * r, 8), :]
                out_ref[4 * position + r, half] = jnp.where(lanes < 64, low, high)


def unpack_kernel(in_ref, out_ref):
    lanes = lane_index()
    for half in range(2):
        for c in range(4):
            left, right = in_ref[2 * c, half], in_ref[2 * c + 1, half]
            cut = pl.ds(128 * c, 128)
            out_ref[0, 2 * half, :, cut] = jnp.where(lanes < 64, left, pltpu.roll(right, 64, 1))
            out_ref[0, 2 * half + 1, :, cut] = jnp.where(lanes < 64, pltpu.roll(left, 64, 1), right)


def call(kernel, shapes, name, specs=None, scratch=(), in_vmem=True, out_vmem=True):
    kind = pltpu.VMEM if out_vmem else jax.ShapeDtypeStruct
    outs = [kind(shape, jnp.float32) for shape in shapes]
    vmem = pl.BlockSpec(memory_space=pltpu.VMEM)
    single = len(outs) == 1

    def run(*args):
        if in_vmem:
            args = [pltpu.with_memory_space_constraint(a, pltpu.VMEM) for a in args]
        return pl.pallas_call(
            kernel,
            out_shape=outs[0] if single else outs,
            in_specs=specs or [vmem] * len(args),
            out_specs=vmem if single else [vmem] * len(outs),
            scratch_shapes=scratch,
            name=name,
        )(*args)

    return run


def groups(count, row_devices, size):
    return [
        [(size * g + q) * row_devices + r for q in range(size) for r in range(row_devices)]
        for g in range(count // size)
    ]


def on_device(start_state, initial_guess, land_mask, bed_class, bed_table):
    count, row_devices = lax.axis_size("tm"), lax.axis_size("rows")
    vmem = pl.BlockSpec(memory_space=pltpu.VMEM)
    smem = pl.BlockSpec(memory_space=pltpu.SMEM)
    packed = call(
        pack_kernel, [(8, FIELDS + 1, *TILE)], "pack", [vmem] * 4 + [smem], in_vmem=False
    )(start_state, initial_guess, land_mask, bed_class, bed_table)
    arrived = lax.all_to_all(packed, AXES, 0, 0, axis_index_groups=groups(count, row_devices, 2))
    state = (FIELDS, 4, *TILE)
    forcing, chain, passed, slopes = call(
        forcing_kernel,
        [(2, *state), (10, *TILE), (2, 10, *TILE), (3, 4, *TILE)],
        "forcing",
        scratch=[pltpu.VMEM((2, FIELDS + 1, 32, 128), jnp.float32)],
    )(arrived)
    to_even = [(i, (i + 2) % count) for i in range(count) if i % 4 >= 2]
    to_next = [(i, i + 4) for i in range(count - 4) if i % 4 < 2]
    chain = lax.ppermute(chain, "tm", to_even)
    passed = lax.ppermute(passed, "tm", to_even)
    chain = call(chain_kernel, [(10, *TILE)], "chain")(chain, forcing, slopes)
    chain = lax.ppermute(chain, "tm", to_next)
    packed = call(
        last_kernel,
        [(16, 2, *TILE)],
        "last",
        scratch=[pltpu.VMEM((4, FIELDS, 32, 128), jnp.float32)],
    )(chain, passed, forcing, slopes)
    arrived = lax.all_to_all(packed, AXES, 0, 0, axis_index_groups=groups(count, row_devices, 4))
    return call(unpack_kernel, [initial_guess.shape], "unpack", out_vmem=False)(arrived)


def solution(mesh):
    in_specs = (
        P(None, "rows", None),
        P("tm", None, "rows", None),
        P("rows", None),
        P("rows", None),
        P(),
    )
    out_specs = P("tm", None, "rows", None)
    return jax.shard_map(
        on_device, mesh=mesh, in_specs=in_specs, out_specs=out_specs, check_vma=False
    )
```

```python
import jax
import jax.numpy as jnp
from jax import lax
from jax.experimental import pallas as pl
from jax.experimental.pallas import tpu as pltpu
from jax.sharding import PartitionSpec as P


FINE_STEPS = 8
FINE = (0.0375, 0.025)
COARSE = (0.3, 0.2)
FIELDS = 4
TILE = (8, 128)
AXES = ("tm", "rows")
RING = 16


def east(x):
    return pltpu.roll(x, 127, 1)


def west(x):
    return pltpu.roll(x, 1, 1)


def north(tiles):
    return [*tiles[1:], pltpu.roll(tiles[0], 7, 0)]


def south(tiles):
    return [pltpu.roll(tiles[3], 1, 0), *tiles[:3]]


def advance(state, statics, ratio, viscous):
    slope_e, slope_n, wet = statics
    half = 0.5 * ratio
    h, p, s, m = state
    inverse = [1.0 / a for a in h]
    u = [a * b for a, b in zip(p, inverse)]
    v = [a * b for a, b in zip(s, inverse)]
    hu = [half * a for a in u]
    hv = [half * a for a in v]
    pressure = [(0.5 * half) * (a * a) for a in h]
    cross = [a * b for a, b in zip(s, hu)]
    east_flux = (
        [half * a for a in p],
        [a * b + c for a, b, c in zip(p, hu, pressure)],
        cross,
        [a * b for a, b in zip(m, hu)],
    )
    north_flux = (
        [half * a for a in s],
        cross,
        [a * b + c for a, b, c in zip(s, hv, pressure)],
        [a * b for a, b in zip(m, hv)],
    )
    moved = []
    for field in range(FIELDS):
        q = state[field]
        near = [viscous * a for a in q]
        up = north([a - b for a, b in zip(near, north_flux[field])])
        down = south([a + b for a, b in zip(near, north_flux[field])])
        tiles = []
        for k in range(4):
            lanes = east(near[k] - east_flux[field][k]) + west(near[k] + east_flux[field][k])
            tiles.append((1.0 - 4.0 * viscous) * q[k] + (lanes + (up[k] + down[k])))
        moved.append(tiles)
    new_p, new_s, new_m = [], [], []
    for k in range(4):
        square = u[k] * u[k] + v[k] * v[k]
        drag = (0.02 * ratio) * jnp.sqrt(square)
        new_p.append(wet[k] * (moved[1][k] - (h[k] * slope_e[k] + drag * u[k])))
        new_s.append(wet[k] * (moved[2][k] - (h[k] * slope_n[k] + drag * v[k])))
        new_m.append(
            moved[3][k] + ((0.05 * ratio) * square - (0.3 * ratio) * (m[k] * inverse[k]))
        )
    return [moved[0], new_p, new_s, new_m]


def scaled(slopes, ratio):
    slope_e, slope_n, wet = slopes
    return [ratio * a for a in slope_e], [ratio * a for a in slope_n], wet


def flat(nested):
    return jax.tree.leaves(nested)


def combine(function, a, b):
    return jax.tree.map(function, a, b)


def read_tiles(ref, *lead):
    return [[ref[(*lead, field, k)] for k in range(4)] for field in range(FIELDS)]


def write_tiles(ref, state, *lead):
    for field in range(FIELDS):
        for k in range(4):
            ref[(*lead, field, k)] = state[field][k]


def lane_index():
    return lax.broadcasted_iota(jnp.int32, TILE, 1)


def pack_kernel(start_ref, guess_ref, mask_ref, class_ref, table_ref, out_ref):
    time_index = lax.axis_index("tm")
    lanes = lane_index()
    use_start = time_index >= lax.axis_size("tm") - 2
    odd = time_index % 2 == 1

    def windows(plane, chunks):
        ahead = [pltpu.roll(a, 32, 1) for a in chunks]
        behind = [pltpu.roll(a, 96, 1) for a in chunks]
        for c in range(4):
            out_ref[2 * c, plane] = jnp.where(lanes < 32, ahead[c - 1], ahead[c])
            out_ref[2 * c + 1, plane] = jnp.where(lanes < 96, behind[c], behind[(c + 1) % 4])

    cuts = [pl.ds(128 * c, 128) for c in range(4)]
    for field in range(FIELDS):
        windows(
            field,
            [jnp.where(use_start, start_ref[field, :, cut], guess_ref[0, field, :, cut]) for cut in cuts],
        )
    static = []
    for cut in cuts:
        classes = class_ref[:, cut]
        bed = jnp.zeros(TILE, jnp.float32)
        for index in range(table_ref.shape[0]):
            bed = jnp.where(classes == index, table_ref[index], bed)
        static.append(jnp.where(odd, mask_ref[:, cut].astype(jnp.float32), bed))
    windows(FIELDS, static)


def fold(ref, state, *lead):
    lanes = lane_index()
    for half in range(2):
        for k in range(4):
            low = pltpu.roll(state[2 * half][k], 96, 1)
            high = pltpu.roll(state[2 * half + 1][k], 32, 1)
            ref[(*lead, 4 * half + k)] = jnp.where(lanes < 64, low, high)
        edge = None
        for slot in range(8):
            tile = state[2 * half + slot // 4][slot % 4]
            left = pltpu.roll(tile, (16 * slot - 24) % 128, 1)
            right = pltpu.roll(tile, (16 * slot + 8 - 96) % 128, 1)
            both = jnp.where(lanes < 16 * slot + 8, left, right)
            edge = both if edge is None else jnp.where(lanes < 16 * slot, edge, both)
        ref[(*lead, 8 + half)] = edge


def unfold(ref, *lead):
    lanes = lane_index()
    state = [[None] * 4 for _ in range(FIELDS)]
    for half in range(2):
        edge = ref[(*lead, 8 + half)]
        for slot in range(8):
            k = slot % 4
            own = pltpu.roll(ref[(*lead, 4 * half + k)], 32 if slot < 4 else 96, 1)
            left = pltpu.roll(edge, (24 - 16 * slot) % 128, 1)
            right = pltpu.roll(edge, (96 - 16 * slot - 8) % 128, 1)
            state[2 * half + slot // 4][k] = jnp.where(
                lanes < 32, left, jnp.where(lanes < 96, own, right)
            )
    return state


def forcing_kernel(in_ref, forcing_ref, chain_ref, pass_ref, slope_ref, rows_ref):
    group = lax.axis_index("tm") // 2
    last = group == lax.axis_size("tm") // 2 - 1
    for pair in range(2):
        for r in range(4):
            for plane in range(FIELDS + 1):
                rows_ref[pair, plane, pl.ds(8 * r, 8), :] = in_ref[4 * pair + r, plane]

    def strided(pair, plane):
        return [rows_ref[pair, plane, pl.ds(k, 8, 4), :] for k in range(4)]

    bed, wet = strided(0, FIELDS), strided(1, FIELDS)
    slope_e = [0.5 * (east(a) - west(a)) for a in bed]
    slope_n = [0.5 * (a - b) for a, b in zip(north(bed), south(bed))]
    slopes = (slope_e, slope_n, wet)
    for index, tiles in enumerate(slopes):
        for k in range(4):
            slope_ref[index, k] = tiles[k]
    fine, coarse = scaled(slopes, FINE[0]), scaled(slopes, COARSE[0])
    first = [[strided(pair, field) for field in range(FIELDS)] for pair in range(2)]
    shape = jax.tree.structure(first)

    def propagate(states):
        def body(_, leaves):
            pairs = jax.tree.unflatten(shape, leaves)
            return tuple(flat([advance(state, fine, *FINE) for state in pairs]))

        return jax.tree.unflatten(shape, lax.fori_loop(0, FINE_STEPS, body, tuple(flat(states))))

    def choose(a, b):
        return combine(lambda x, y: jnp.where(last, x, y), a, b)

    before = propagate(first)
    before[0] = choose(first[0], before[0])
    reached = propagate(before)
    forcing = [
        combine(jnp.subtract, reached[pair], advance(before[pair], coarse, *COARSE))
        for pair in range(2)
    ]
    second = combine(jnp.add, advance(reached[0], coarse, *COARSE), forcing[1])
    fold(chain_ref, second)
    fold(pass_ref, choose(reached[0], forcing[0]), 0)
    fold(pass_ref, choose(second, forcing[1]), 1)
    for pair in range(2):
        write_tiles(forcing_ref, forcing[pair], pair)


def coarse_of(slope_ref):
    return scaled([[slope_ref[index, k] for k in range(4)] for index in range(3)], COARSE[0])


def relax(opening, forcing, coarse):
    return combine(jnp.add, advance(opening, coarse, *COARSE), forcing)


def chain_kernel(in_ref, forcing_ref, slope_ref, out_ref):
    coarse = coarse_of(slope_ref)
    value = unfold(in_ref)
    for pair in range(2):
        value = relax(value, read_tiles(forcing_ref, pair), coarse)
    fold(out_ref, value)


def late_chain_kernel(in_ref, forcing_ref, slope_ref, order_ref, out_ref):
    del order_ref
    chain_kernel(in_ref, forcing_ref, slope_ref, out_ref)


def last_kernel(
    in_ref, late_ref, across_ref, pass_ref, forcing_ref, slope_ref, out_ref, join_ref, rows_ref
):
    lanes = lane_index()
    opens = lax.axis_index("tm") < 2
    coarse = coarse_of(slope_ref)
    place = lax.axis_index("tm") % RING // 2
    for tile in range(10):
        joined = jnp.where(place == 2, late_ref[tile], in_ref[tile])
        join_ref[tile] = jnp.where(place == 0, across_ref[tile], joined)
    value = unfold(join_ref)
    for position in range(4):
        if position < 2:
            given = unfold(pass_ref, position)
            value = combine(
                lambda a, b: jnp.where(opens, a, b), given, relax(value, given, coarse)
            )
        else:
            value = relax(value, read_tiles(forcing_ref, position - 2), coarse)
        for field in range(FIELDS):
            shift = 96 if field % 2 == 0 else 32
            for k in range(4):
                rows_ref[position, field, pl.ds(k, 8, 4), :] = pltpu.roll(value[field][k], shift, 1)
        for r in range(4):
            for half in range(2):
                low = rows_ref[position, 2 * half, pl.ds(8 * r, 8), :]
                high = rows_ref[position, 2 * half + 1, pl.ds(8 * r, 8), :]
                out_ref[4 * position + r, half] = jnp.where(lanes < 64, low, high)


def unpack_kernel(in_ref, out_ref):
    lanes = lane_index()
    for half in range(2):
        for c in range(4):
            left, right = in_ref[2 * c, half], in_ref[2 * c + 1, half]
            cut = pl.ds(128 * c, 128)
            out_ref[0, 2 * half, :, cut] = jnp.where(lanes < 64, left, pltpu.roll(right, 64, 1))
            out_ref[0, 2 * half + 1, :, cut] = jnp.where(lanes < 64, pltpu.roll(left, 64, 1), right)


def call(kernel, shapes, specs=None, scratch=(), in_vmem=True, out_vmem=True):
    kind = pltpu.VMEM if out_vmem else jax.ShapeDtypeStruct
    outs = [kind(shape, jnp.float32) for shape in shapes]
    vmem = pl.BlockSpec(memory_space=pltpu.VMEM)
    single = len(outs) == 1

    def run(*args):
        if in_vmem:
            args = [pltpu.with_memory_space_constraint(a, pltpu.VMEM) for a in args]
        return pl.pallas_call(
            kernel,
            out_shape=outs[0] if single else outs,
            in_specs=specs or [vmem] * len(args),
            out_specs=vmem if single else [vmem] * len(outs),
            scratch_shapes=scratch,
        )(*args)

    return run


def groups(count, row_devices, size):
    return [
        [(size * g + q) * row_devices + r for q in range(size) for r in range(row_devices)]
        for g in range(count // size)
    ]


def on_device(start_state, initial_guess, land_mask, bed_class, bed_table):
    count, row_devices = lax.axis_size("tm"), lax.axis_size("rows")
    vmem = pl.BlockSpec(memory_space=pltpu.VMEM)
    smem = pl.BlockSpec(memory_space=pltpu.SMEM)
    packed = call(
        pack_kernel, [(8, FIELDS + 1, *TILE)], [vmem] * 4 + [smem], in_vmem=False
    )(start_state, initial_guess, land_mask, bed_class, bed_table)
    arrived = lax.all_to_all(packed, AXES, 0, 0, axis_index_groups=groups(count, row_devices, 2))
    state = (FIELDS, 4, *TILE)
    forcing, chain, passed, slopes = call(
        forcing_kernel,
        [(2, *state), (10, *TILE), (2, 10, *TILE), (3, 4, *TILE)],
        scratch=[pltpu.VMEM((2, FIELDS + 1, 32, 128), jnp.float32)],
    )(arrived)
    to_even = [(i, (i + 2) % count) for i in range(count) if i % 4 >= 2]
    to_next = [(i, i + 4) for i in range(count - 4) if i % 4 < 2]
    inside = [(i, j) for i, j in to_even if i % RING < RING - 2]
    crossing = [(i, j) for i, j in to_even if i % RING >= RING - 2]
    handed_across = [(i, j) for i, j in to_next if i % RING >= RING - 4]
    handed_late = [(i, j) for i, j in to_next if i % RING < 2]
    handed_inside = [(i, j) for i, j in to_next if 2 <= i % RING < RING - 4]
    first = lax.ppermute(chain, "tm", inside)
    second = lax.ppermute(chain, "tm", crossing)
    passed = lax.ppermute(passed, "tm", to_even)
    first = call(chain_kernel, [(10, *TILE)])(first, forcing, slopes)
    second = call(late_chain_kernel, [(10, *TILE)])(second, forcing, slopes, first)
    across = lax.ppermute(first, "tm", handed_across)
    second = lax.ppermute(second, "tm", handed_late)
    first = lax.ppermute(first, "tm", handed_inside)
    packed = call(
        last_kernel,
        [(16, 2, *TILE)],
        scratch=[pltpu.VMEM((10, *TILE), jnp.float32), pltpu.VMEM((4, FIELDS, 32, 128), jnp.float32)],
    )(first, second, across, passed, forcing, slopes)
    arrived = lax.all_to_all(packed, AXES, 0, 0, axis_index_groups=groups(count, row_devices, 4))
    return call(unpack_kernel, [initial_guess.shape], out_vmem=False)(arrived)


def solution(mesh):
    in_specs = (
        P(None, "rows", None),
        P("tm", None, "rows", None),
        P("rows", None),
        P("rows", None),
        P(),
    )
    out_specs = P("tm", None, "rows", None)
    return jax.shard_map(
        on_device, mesh=mesh, in_specs=in_specs, out_specs=out_specs, check_vma=False
    )
```

```python
import jax
import jax.numpy as jnp
from jax import lax
from jax.experimental import pallas as pl
from jax.experimental.pallas import tpu as pltpu
from jax.sharding import PartitionSpec as P


FINE_STEPS = 8
FINE = (0.0375, 0.025)
COARSE = (0.3, 0.2)
FIELDS = 4
TILE = (8, 128)
AXES = ("tm", "rows")
RING = 16


def east(x):
    return pltpu.roll(x, 127, 1)


def west(x):
    return pltpu.roll(x, 1, 1)


def north(tiles):
    return [*tiles[1:], pltpu.roll(tiles[0], 7, 0)]


def south(tiles):
    return [pltpu.roll(tiles[3], 1, 0), *tiles[:3]]


def advance(state, statics, ratio, viscous):
    slope_e, slope_n, wet = statics
    half = 0.5 * ratio
    h, p, s, m = state
    inverse = [1.0 / a for a in h]
    u = [a * b for a, b in zip(p, inverse)]
    v = [a * b for a, b in zip(s, inverse)]
    hu = [half * a for a in u]
    hv = [half * a for a in v]
    pressure = [(0.5 * half) * (a * a) for a in h]
    cross = [a * b for a, b in zip(s, hu)]
    east_flux = (
        [half * a for a in p],
        [a * b + c for a, b, c in zip(p, hu, pressure)],
        cross,
        [a * b for a, b in zip(m, hu)],
    )
    north_flux = (
        [half * a for a in s],
        cross,
        [a * b + c for a, b, c in zip(s, hv, pressure)],
        [a * b for a, b in zip(m, hv)],
    )
    moved = []
    for field in range(FIELDS):
        q = state[field]
        near = [viscous * a for a in q]
        up = north([a - b for a, b in zip(near, north_flux[field])])
        down = south([a + b for a, b in zip(near, north_flux[field])])
        tiles = []
        for k in range(4):
            lanes = east(near[k] - east_flux[field][k]) + west(near[k] + east_flux[field][k])
            tiles.append((1.0 - 4.0 * viscous) * q[k] + (lanes + (up[k] + down[k])))
        moved.append(tiles)
    new_p, new_s, new_m = [], [], []
    for k in range(4):
        square = u[k] * u[k] + v[k] * v[k]
        drag = (0.02 * ratio) * jnp.sqrt(square)
        new_p.append(wet[k] * (moved[1][k] - (h[k] * slope_e[k] + drag * u[k])))
        new_s.append(wet[k] * (moved[2][k] - (h[k] * slope_n[k] + drag * v[k])))
        new_m.append(
            moved[3][k] + ((0.05 * ratio) * square - (0.3 * ratio) * (m[k] * inverse[k]))
        )
    return [moved[0], new_p, new_s, new_m]


def scaled(slopes, ratio):
    slope_e, slope_n, wet = slopes
    return [ratio * a for a in slope_e], [ratio * a for a in slope_n], wet


def flat(nested):
    return jax.tree.leaves(nested)


def combine(function, a, b):
    return jax.tree.map(function, a, b)


def read_tiles(ref, *lead):
    return [[ref[(*lead, field, k)] for k in range(4)] for field in range(FIELDS)]


def write_tiles(ref, state, *lead):
    for field in range(FIELDS):
        for k in range(4):
            ref[(*lead, field, k)] = state[field][k]


def lane_index():
    return lax.broadcasted_iota(jnp.int32, TILE, 1)


def pack_kernel(start_ref, guess_ref, mask_ref, class_ref, table_ref, out_ref):
    time_index = lax.axis_index("tm")
    lanes = lane_index()
    use_start = time_index >= lax.axis_size("tm") - 2
    odd = time_index % 2 == 1

    def windows(plane, chunks):
        ahead = [pltpu.roll(a, 32, 1) for a in chunks]
        behind = [pltpu.roll(a, 96, 1) for a in chunks]
        for c in range(4):
            out_ref[2 * c, plane] = jnp.where(lanes < 32, ahead[c - 1], ahead[c])
            out_ref[2 * c + 1, plane] = jnp.where(lanes < 96, behind[c], behind[(c + 1) % 4])

    cuts = [pl.ds(128 * c, 128) for c in range(4)]
    for field in range(FIELDS):
        windows(
            field,
            [jnp.where(use_start, start_ref[field, :, cut], guess_ref[0, field, :, cut]) for cut in cuts],
        )
    static = []
    for cut in cuts:
        classes = class_ref[:, cut]
        bed = jnp.zeros(TILE, jnp.float32)
        for index in range(table_ref.shape[0]):
            bed = jnp.where(classes == index, table_ref[index], bed)
        static.append(jnp.where(odd, mask_ref[:, cut].astype(jnp.float32), bed))
    windows(FIELDS, static)


def fold(ref, state, *lead):
    lanes = lane_index()
    for half in range(2):
        for k in range(4):
            low = pltpu.roll(state[2 * half][k], 96, 1)
            high = pltpu.roll(state[2 * half + 1][k], 32, 1)
            ref[(*lead, 4 * half + k)] = jnp.where(lanes < 64, low, high)
        edge = None
        for slot in range(8):
            tile = state[2 * half + slot // 4][slot % 4]
            left = pltpu.roll(tile, (16 * slot - 24) % 128, 1)
            right = pltpu.roll(tile, (16 * slot + 8 - 96) % 128, 1)
            both = jnp.where(lanes < 16 * slot + 8, left, right)
            edge = both if edge is None else jnp.where(lanes < 16 * slot, edge, both)
        ref[(*lead, 8 + half)] = edge


def unfold(ref, *lead):
    lanes = lane_index()
    state = [[None] * 4 for _ in range(FIELDS)]
    for half in range(2):
        edge = ref[(*lead, 8 + half)]
        for slot in range(8):
            k = slot % 4
            own = pltpu.roll(ref[(*lead, 4 * half + k)], 32 if slot < 4 else 96, 1)
            left = pltpu.roll(edge, (24 - 16 * slot) % 128, 1)
            right = pltpu.roll(edge, (96 - 16 * slot - 8) % 128, 1)
            state[2 * half + slot // 4][k] = jnp.where(
                lanes < 32, left, jnp.where(lanes < 96, own, right)
            )
    return state


def forcing_kernel(in_ref, forcing_ref, chain_ref, pass_ref, slope_ref, rows_ref):
    group = lax.axis_index("tm") // 2
    last = group == lax.axis_size("tm") // 2 - 1
    for pair in range(2):
        for r in range(4):
            for plane in range(FIELDS + 1):
                rows_ref[pair, plane, pl.ds(8 * r, 8), :] = in_ref[4 * pair + r, plane]

    def strided(pair, plane):
        return [rows_ref[pair, plane, pl.ds(k, 8, 4), :] for k in range(4)]

    bed, wet = strided(0, FIELDS), strided(1, FIELDS)
    slope_e = [0.5 * (east(a) - west(a)) for a in bed]
    slope_n = [0.5 * (a - b) for a, b in zip(north(bed), south(bed))]
    slopes = (slope_e, slope_n, wet)
    for index, tiles in enumerate(slopes):
        for k in range(4):
            slope_ref[index, k] = tiles[k]
    fine, coarse = scaled(slopes, FINE[0]), scaled(slopes, COARSE[0])
    first = [[strided(pair, field) for field in range(FIELDS)] for pair in range(2)]
    shape = jax.tree.structure(first)

    def propagate(states):
        def body(_, leaves):
            pairs = jax.tree.unflatten(shape, leaves)
            return tuple(flat([advance(state, fine, *FINE) for state in pairs]))

        return jax.tree.unflatten(shape, lax.fori_loop(0, FINE_STEPS, body, tuple(flat(states))))

    def choose(a, b):
        return combine(lambda x, y: jnp.where(last, x, y), a, b)

    before = propagate(first)
    before[0] = choose(first[0], before[0])
    reached = propagate(before)
    forcing = [
        combine(jnp.subtract, reached[pair], advance(before[pair], coarse, *COARSE))
        for pair in range(2)
    ]
    second = combine(jnp.add, advance(reached[0], coarse, *COARSE), forcing[1])
    fold(chain_ref, second)
    fold(pass_ref, choose(reached[0], forcing[0]), 0)
    fold(pass_ref, choose(second, forcing[1]), 1)
    for pair in range(2):
        write_tiles(forcing_ref, forcing[pair], pair)


def coarse_of(slope_ref):
    return scaled([[slope_ref[index, k] for k in range(4)] for index in range(3)], COARSE[0])


def relax(opening, forcing, coarse):
    return combine(jnp.add, advance(opening, coarse, *COARSE), forcing)


def last_kernel(
    far_ref, far_across_ref, middle_ref, middle_across_ref, pass_ref, forcing_ref, slope_ref,
    out_ref, far_join_ref, middle_join_ref, rows_ref,
):
    starts = lax.axis_index("tm") % RING < 2
    for tile in range(10):
        far_join_ref[tile] = jnp.where(starts, far_across_ref[tile], far_ref[tile])
        for pair in range(2):
            middle_join_ref[pair, tile] = jnp.where(
                starts, middle_across_ref[pair, tile], middle_ref[pair, tile]
            )
    lanes = lane_index()
    opens = lax.axis_index("tm") < 2
    coarse = coarse_of(slope_ref)
    value = unfold(far_join_ref)
    for pair in range(2):
        value = relax(value, unfold(middle_join_ref, pair), coarse)
    for position in range(4):
        if position < 2:
            given = unfold(pass_ref, position)
            value = combine(
                lambda a, b: jnp.where(opens, a, b), given, relax(value, given, coarse)
            )
        else:
            value = relax(value, read_tiles(forcing_ref, position - 2), coarse)
        for field in range(FIELDS):
            shift = 96 if field % 2 == 0 else 32
            for k in range(4):
                rows_ref[position, field, pl.ds(k, 8, 4), :] = pltpu.roll(value[field][k], shift, 1)
        for r in range(4):
            for half in range(2):
                low = rows_ref[position, 2 * half, pl.ds(8 * r, 8), :]
                high = rows_ref[position, 2 * half + 1, pl.ds(8 * r, 8), :]
                out_ref[4 * position + r, half] = jnp.where(lanes < 64, low, high)


def unpack_kernel(in_ref, out_ref):
    lanes = lane_index()
    for half in range(2):
        for c in range(4):
            left, right = in_ref[2 * c, half], in_ref[2 * c + 1, half]
            cut = pl.ds(128 * c, 128)
            out_ref[0, 2 * half, :, cut] = jnp.where(lanes < 64, left, pltpu.roll(right, 64, 1))
            out_ref[0, 2 * half + 1, :, cut] = jnp.where(lanes < 64, pltpu.roll(left, 64, 1), right)


def call(kernel, shapes, specs=None, scratch=(), in_vmem=True, out_vmem=True):
    kind = pltpu.VMEM if out_vmem else jax.ShapeDtypeStruct
    outs = [kind(shape, jnp.float32) for shape in shapes]
    vmem = pl.BlockSpec(memory_space=pltpu.VMEM)
    single = len(outs) == 1

    def run(*args):
        if in_vmem:
            args = [pltpu.with_memory_space_constraint(a, pltpu.VMEM) for a in args]
        return pl.pallas_call(
            kernel,
            out_shape=outs[0] if single else outs,
            in_specs=specs or [vmem] * len(args),
            out_specs=vmem if single else [vmem] * len(outs),
            scratch_shapes=scratch,
        )(*args)

    return run


def groups(count, row_devices, size):
    return [
        [(size * g + q) * row_devices + r for q in range(size) for r in range(row_devices)]
        for g in range(count // size)
    ]


def on_device(start_state, initial_guess, land_mask, bed_class, bed_table):
    count, row_devices = lax.axis_size("tm"), lax.axis_size("rows")
    vmem = pl.BlockSpec(memory_space=pltpu.VMEM)
    smem = pl.BlockSpec(memory_space=pltpu.SMEM)
    packed = call(
        pack_kernel, [(8, FIELDS + 1, *TILE)], [vmem] * 4 + [smem], in_vmem=False
    )(start_state, initial_guess, land_mask, bed_class, bed_table)
    arrived = lax.all_to_all(packed, AXES, 0, 0, axis_index_groups=groups(count, row_devices, 2))
    state = (FIELDS, 4, *TILE)
    forcing, chain, passed, slopes = call(
        forcing_kernel,
        [(2, *state), (10, *TILE), (2, 10, *TILE), (3, 4, *TILE)],
        scratch=[pltpu.VMEM((2, FIELDS + 1, 32, 128), jnp.float32)],
    )(arrived)
    even = [i for i in range(count) if i % 4 < 2]
    odd = [i for i in range(count) if i % 4 >= 2]
    two = [(i, (i + 2) % count) for i in odd]
    four = [(i, i + 4) for i in even if i + 4 < count]
    six = [(i, (i + 6) % count) for i in odd if i < count - 6 or i >= count - 2]

    def send(value, pairs):
        return lax.ppermute(value, "tm", pairs)

    far_across = send(chain, [(i, j) for i, j in six if j % RING < 2])
    middle_across = send(passed, [(i, j) for i, j in four if j % RING < 2])
    near = send(passed, two)
    far = send(chain, [(i, j) for i, j in six if j % RING >= 2])
    middle = send(passed, [(i, j) for i, j in four if j % RING >= 2])
    packed = call(
        last_kernel,
        [(16, 2, *TILE)],
        scratch=[
            pltpu.VMEM((10, *TILE), jnp.float32),
            pltpu.VMEM((2, 10, *TILE), jnp.float32),
            pltpu.VMEM((4, FIELDS, 32, 128), jnp.float32),
        ],
    )(far, far_across, middle, middle_across, near, forcing, slopes)
    arrived = lax.all_to_all(packed, AXES, 0, 0, axis_index_groups=groups(count, row_devices, 4))
    return call(unpack_kernel, [initial_guess.shape], out_vmem=False)(arrived)


def solution(mesh):
    in_specs = (
        P(None, "rows", None),
        P("tm", None, "rows", None),
        P("rows", None),
        P("rows", None),
        P(),
    )
    out_specs = P("tm", None, "rows", None)
    return jax.shard_map(
        on_device, mesh=mesh, in_specs=in_specs, out_specs=out_specs, check_vma=False
    )
```

```python
import jax
import jax.numpy as jnp
from jax import lax
from jax.experimental import pallas as pl
from jax.experimental.pallas import tpu as pltpu
from jax.sharding import PartitionSpec as P


FINE_STEPS = 8
FINE = (0.0375, 0.025)
COARSE = (0.3, 0.2)
FIELDS = 4
TILE = (8, 128)
AXES = ("tm", "rows")
SMALLEST = 1.1754944e-38
RING = 16


def east(x):
    return pltpu.roll(x, 127, 1)


def west(x):
    return pltpu.roll(x, 1, 1)


def north(tiles):
    return [*tiles[1:], pltpu.roll(tiles[0], 7, 0)]


def south(tiles):
    return [pltpu.roll(tiles[3], 1, 0), *tiles[:3]]


def advance(state, statics, ratio, viscous):
    slope_e, slope_n, wet = statics
    half = 0.5 * ratio
    h, p, s, m = state
    inverse = [half / a for a in h]
    u = [a * b for a, b in zip(p, inverse)]
    v = [a * b for a, b in zip(s, inverse)]
    pressure = [(0.5 * half) * (a * a) for a in h]
    cross = [a * b for a, b in zip(s, u)]
    east_flux = (
        [half * a for a in p],
        [a * b + c for a, b, c in zip(p, u, pressure)],
        cross,
        [a * b for a, b in zip(m, u)],
    )
    north_flux = (
        [half * a for a in s],
        cross,
        [a * b + c for a, b, c in zip(s, v, pressure)],
        [a * b for a, b in zip(m, v)],
    )
    moved = []
    for field in range(FIELDS):
        q = state[field]
        near = [viscous * a for a in q]
        up = north([a - b for a, b in zip(near, north_flux[field])])
        down = south([a + b for a, b in zip(near, north_flux[field])])
        tiles = []
        for k in range(4):
            lanes = east(near[k] - east_flux[field][k]) + west(near[k] + east_flux[field][k])
            tiles.append((1.0 - 4.0 * viscous) * q[k] + (lanes + (up[k] + down[k])))
        moved.append(tiles)
    new_p, new_s, new_m = [], [], []
    for k in range(4):
        square = u[k] * u[k] + v[k] * v[k]
        root = square * lax.rsqrt(jnp.maximum(square, SMALLEST))
        drag = (0.02 * ratio / half**2) * root
        new_p.append(wet[k] * (moved[1][k] - (h[k] * slope_e[k] + drag * u[k])))
        new_s.append(wet[k] * (moved[2][k] - (h[k] * slope_n[k] + drag * v[k])))
        settled = (0.3 * ratio / half) * (m[k] * inverse[k])
        new_m.append(moved[3][k] + ((0.05 * ratio / half**2) * square - settled))
    return [moved[0], new_p, new_s, new_m]


def scaled(slopes, ratio):
    slope_e, slope_n, wet = slopes
    return [ratio * a for a in slope_e], [ratio * a for a in slope_n], wet


def flat(nested):
    return jax.tree.leaves(nested)


def combine(function, a, b):
    return jax.tree.map(function, a, b)


def read_tiles(ref, *lead):
    return [[ref[(*lead, field, k)] for k in range(4)] for field in range(FIELDS)]


def write_tiles(ref, state, *lead):
    for field in range(FIELDS):
        for k in range(4):
            ref[(*lead, field, k)] = state[field][k]


def lane_index():
    return lax.broadcasted_iota(jnp.int32, TILE, 1)


def pack_kernel(start_ref, guess_ref, mask_ref, class_ref, table_ref, out_ref):
    time_index = lax.axis_index("tm")
    lanes = lane_index()
    use_start = time_index >= lax.axis_size("tm") - 2
    odd = time_index % 2 == 1

    def windows(plane, chunks):
        ahead = [pltpu.roll(a, 32, 1) for a in chunks]
        behind = [pltpu.roll(a, 96, 1) for a in chunks]
        for c in range(4):
            out_ref[2 * c, plane] = jnp.where(lanes < 32, ahead[c - 1], ahead[c])
            out_ref[2 * c + 1, plane] = jnp.where(lanes < 96, behind[c], behind[(c + 1) % 4])

    cuts = [pl.ds(128 * c, 128) for c in range(4)]
    for field in range(FIELDS):
        windows(
            field,
            [jnp.where(use_start, start_ref[field, :, cut], guess_ref[0, field, :, cut]) for cut in cuts],
        )
    static = []
    for cut in cuts:
        classes = class_ref[:, cut]
        bed = jnp.zeros(TILE, jnp.float32)
        for index in range(table_ref.shape[0]):
            bed = jnp.where(classes == index, table_ref[index], bed)
        static.append(jnp.where(odd, mask_ref[:, cut].astype(jnp.float32), bed))
    windows(FIELDS, static)


SLOTS = {5: 11, 7: 8}
DIVIDE = {5: 205, 7: 147}


def payload(states, width):
    return 8 * states - (-16 * states // SLOTS[width])


def slot_of_lane(width):
    lanes = lane_index()
    right = ((lanes - 64) * DIVIDE[width]) >> 10
    left = (lanes * DIVIDE[width]) >> 10
    inside = jnp.where(lanes < 64, left + 1, right)
    return jnp.where(lanes >= 128 - width, 0, inside)


def fold(ref, states, width):
    lanes, slots = lane_index(), slot_of_lane(width)
    edges = [None] * (payload(len(states), width) - 8 * len(states))
    for index, state in enumerate(states):
        for k in range(4):
            for half in range(2):
                low = pltpu.roll(state[2 * half][k], 96, 1)
                high = pltpu.roll(state[2 * half + 1][k], 32, 1)
                ref[8 * index + 4 * half + k] = jnp.where(lanes < 64, low, high)
                for part, turned in enumerate((low, high)):
                    number = 16 * index + 4 * (2 * half + part) + k
                    edge, slot = divmod(number, SLOTS[width])
                    shift = (64 * part + width * slot) % 128
                    moved = pltpu.roll(turned, shift, 1) if shift else turned
                    edges[edge] = (
                        moved
                        if edges[edge] is None
                        else jnp.where(slots == slot, moved, edges[edge])
                    )
    for index, edge in enumerate(edges):
        ref[8 * len(states) + index] = edge


def unfold(ref, states, width, index=0):
    lanes = lane_index()
    own_lanes = (lanes >= 32) & (lanes < 96)
    state = [[None] * 4 for _ in range(FIELDS)]
    for field in range(FIELDS):
        for k in range(4):
            main = ref[8 * index + 4 * (field // 2) + k]
            own = pltpu.roll(main, 32 if field % 2 == 0 else 96, 1)
            edge, slot = divmod(16 * index + 4 * field + k, SLOTS[width])
            edge = ref[8 * states + edge]
            shift = (32 - width * slot) % 128
            state[field][k] = jnp.where(own_lanes, own, pltpu.roll(edge, shift, 1))
    return state


def forcing_kernel(in_ref, forcing_ref, chain_ref, pass_ref, slope_ref, rows_ref):
    group = lax.axis_index("tm") // 2
    last = group == lax.axis_size("tm") // 2 - 1
    for pair in range(2):
        for r in range(4):
            for plane in range(FIELDS + 1):
                rows_ref[pair, plane, pl.ds(8 * r, 8), :] = in_ref[4 * pair + r, plane]

    def strided(pair, plane):
        return [rows_ref[pair, plane, pl.ds(k, 8, 4), :] for k in range(4)]

    bed, wet = strided(0, FIELDS), strided(1, FIELDS)
    slope_e = [0.5 * (east(a) - west(a)) for a in bed]
    slope_n = [0.5 * (a - b) for a, b in zip(north(bed), south(bed))]
    slopes = (slope_e, slope_n, wet)
    for index, tiles in enumerate(slopes):
        for k in range(4):
            slope_ref[index, k] = tiles[k]
    fine, coarse = scaled(slopes, FINE[0]), scaled(slopes, COARSE[0])
    first = [[strided(pair, field) for field in range(FIELDS)] for pair in range(2)]
    shape = jax.tree.structure(first)

    def propagate(states):
        def body(_, leaves):
            pairs = jax.tree.unflatten(shape, leaves)
            return tuple(flat([advance(state, fine, *FINE) for state in pairs]))

        return jax.tree.unflatten(shape, lax.fori_loop(0, FINE_STEPS, body, tuple(flat(states)), unroll=8))

    def choose(a, b):
        return combine(lambda x, y: jnp.where(last, x, y), a, b)

    before = propagate(first)
    before[0] = choose(first[0], before[0])
    reached = propagate(before)
    forcing = [
        combine(jnp.subtract, reached[pair], advance(before[pair], coarse, *COARSE))
        for pair in range(2)
    ]
    second = combine(jnp.add, advance(reached[0], coarse, *COARSE), forcing[1])
    fold(chain_ref, [second], 7)
    fold(pass_ref, [choose(reached[0], forcing[0]), choose(second, forcing[1])], 5)
    for pair in range(2):
        write_tiles(forcing_ref, forcing[pair], pair)


def coarse_of(slope_ref):
    return scaled([[slope_ref[index, k] for k in range(4)] for index in range(3)], COARSE[0])


def relax(opening, forcing, coarse):
    return combine(jnp.add, advance(opening, coarse, *COARSE), forcing)


def last_kernel(
    far_ref, far_across_ref, middle_ref, middle_across_ref, pass_ref, forcing_ref, slope_ref,
    out_ref, far_join_ref, middle_join_ref, rows_ref,
):
    starts = lax.axis_index("tm") % RING < 2
    for tile in range(far_ref.shape[0]):
        far_join_ref[tile] = jnp.where(starts, far_across_ref[tile], far_ref[tile])
    for tile in range(middle_ref.shape[0]):
        middle_join_ref[tile] = jnp.where(starts, middle_across_ref[tile], middle_ref[tile])
    lanes = lane_index()
    opens = lax.axis_index("tm") < 2
    coarse = coarse_of(slope_ref)
    value = unfold(far_join_ref, 1, 7)
    for pair in range(2):
        value = relax(value, unfold(middle_join_ref, 2, 5, pair), coarse)
    for position in range(4):
        if position < 2:
            given = unfold(pass_ref, 2, 5, position)
            value = combine(
                lambda a, b: jnp.where(opens, a, b), given, relax(value, given, coarse)
            )
        else:
            value = relax(value, read_tiles(forcing_ref, position - 2), coarse)
        for field in range(FIELDS):
            shift = 96 if field % 2 == 0 else 32
            for k in range(4):
                rows_ref[position, field, pl.ds(k, 8, 4), :] = pltpu.roll(value[field][k], shift, 1)
        for r in range(4):
            for half in range(2):
                low = rows_ref[position, 2 * half, pl.ds(8 * r, 8), :]
                high = rows_ref[position, 2 * half + 1, pl.ds(8 * r, 8), :]
                out_ref[4 * position + r, half] = jnp.where(lanes < 64, low, high)


def unpack_kernel(in_ref, out_ref):
    lanes = lane_index()
    for half in range(2):
        for c in range(4):
            left, right = in_ref[2 * c, half], in_ref[2 * c + 1, half]
            cut = pl.ds(128 * c, 128)
            out_ref[0, 2 * half, :, cut] = jnp.where(lanes < 64, left, pltpu.roll(right, 64, 1))
            out_ref[0, 2 * half + 1, :, cut] = jnp.where(lanes < 64, pltpu.roll(left, 64, 1), right)


def call(kernel, shapes, specs=None, scratch=(), in_vmem=True, out_vmem=True):
    kind = pltpu.VMEM if out_vmem else jax.ShapeDtypeStruct
    outs = [kind(shape, jnp.float32) for shape in shapes]
    vmem = pl.BlockSpec(memory_space=pltpu.VMEM)
    single = len(outs) == 1

    def run(*args):
        if in_vmem:
            args = [pltpu.with_memory_space_constraint(a, pltpu.VMEM) for a in args]
        return pl.pallas_call(
            kernel,
            out_shape=outs[0] if single else outs,
            in_specs=specs or [vmem] * len(args),
            out_specs=vmem if single else [vmem] * len(outs),
            scratch_shapes=scratch,
        )(*args)

    return run


def groups(count, row_devices, size):
    return [
        [(size * g + q) * row_devices + r for q in range(size) for r in range(row_devices)]
        for g in range(count // size)
    ]


def on_device(start_state, initial_guess, land_mask, bed_class, bed_table):
    count, row_devices = lax.axis_size("tm"), lax.axis_size("rows")
    vmem = pl.BlockSpec(memory_space=pltpu.VMEM)
    smem = pl.BlockSpec(memory_space=pltpu.SMEM)
    packed = call(
        pack_kernel, [(8, FIELDS + 1, *TILE)], [vmem] * 4 + [smem], in_vmem=False
    )(start_state, initial_guess, land_mask, bed_class, bed_table)
    arrived = lax.all_to_all(packed, AXES, 0, 0, axis_index_groups=groups(count, row_devices, 2))
    state = (FIELDS, 4, *TILE)
    forcing, chain, passed, slopes = call(
        forcing_kernel,
        [(2, *state), (payload(1, 7), *TILE), (payload(2, 5), *TILE), (3, 4, *TILE)],
        scratch=[pltpu.VMEM((2, FIELDS + 1, 32, 128), jnp.float32)],
    )(arrived)
    even = [i for i in range(count) if i % 4 < 2]
    odd = [i for i in range(count) if i % 4 >= 2]
    two = [(i, (i + 2) % count) for i in odd]
    four = [(i, i + 4) for i in even if i + 4 < count]
    six = [(i, (i + 6) % count) for i in odd if i < count - 6 or i >= count - 2]

    def send(value, pairs):
        return lax.ppermute(value, "tm", pairs)

    far_across = send(chain, [(i, j) for i, j in six if j % RING < 2])
    middle_across = send(passed, [(i, j) for i, j in four if j % RING < 2])
    near = send(passed, two)
    far = send(chain, [(i, j) for i, j in six if j % RING >= 2])
    middle = send(passed, [(i, j) for i, j in four if j % RING >= 2])
    packed = call(
        last_kernel,
        [(16, 2, *TILE)],
        scratch=[
            pltpu.VMEM((payload(1, 7), *TILE), jnp.float32),
            pltpu.VMEM((payload(2, 5), *TILE), jnp.float32),
            pltpu.VMEM((4, FIELDS, 32, 128), jnp.float32),
        ],
    )(far, far_across, middle, middle_across, near, forcing, slopes)
    arrived = lax.all_to_all(packed, AXES, 0, 0, axis_index_groups=groups(count, row_devices, 4))
    return call(unpack_kernel, [initial_guess.shape], out_vmem=False)(arrived)


def solution(mesh):
    in_specs = (
        P(None, "rows", None),
        P("tm", None, "rows", None),
        P("rows", None),
        P("rows", None),
        P(),
    )
    out_specs = P("tm", None, "rows", None)
    return jax.shard_map(
        on_device, mesh=mesh, in_specs=in_specs, out_specs=out_specs, check_vma=False
    )
```

```python
import jax
import jax.numpy as jnp
from jax import lax
from jax.experimental import pallas as pl
from jax.experimental.pallas import tpu as pltpu
from jax.sharding import PartitionSpec as P


FINE_STEPS = 8
FINE = (0.0375, 0.025)
COARSE = (0.3, 0.2)
FIELDS = 4
TILE = (8, 128)
AXES = ("tm", "rows")
SMALLEST = 1.1754944e-38
RING = 16


def east(x):
    return pltpu.roll(x, 127, 1)


def west(x):
    return pltpu.roll(x, 1, 1)


def north(tiles):
    return [*tiles[1:], pltpu.roll(tiles[0], 7, 0)]


def south(tiles):
    return [pltpu.roll(tiles[3], 1, 0), *tiles[:3]]


def advance(state, statics, ratio, viscous):
    slope_e, slope_n, wet = statics
    half = 0.5 * ratio
    h, p, s, m = state
    inverse = [half / a for a in h]
    u = [a * b for a, b in zip(p, inverse)]
    v = [a * b for a, b in zip(s, inverse)]
    pressure = [(0.5 * half) * (a * a) for a in h]
    cross = [a * b for a, b in zip(s, u)]
    east_flux = (
        [half * a for a in p],
        [a * b + c for a, b, c in zip(p, u, pressure)],
        cross,
        [a * b for a, b in zip(m, u)],
    )
    north_flux = (
        [half * a for a in s],
        cross,
        [a * b + c for a, b, c in zip(s, v, pressure)],
        [a * b for a, b in zip(m, v)],
    )
    moved = []
    for field in range(FIELDS):
        q = state[field]
        near = [viscous * a for a in q]
        up = north([a - b for a, b in zip(near, north_flux[field])])
        down = south([a + b for a, b in zip(near, north_flux[field])])
        tiles = []
        for k in range(4):
            lanes = east(near[k] - east_flux[field][k]) + west(near[k] + east_flux[field][k])
            tiles.append((1.0 - 4.0 * viscous) * q[k] + (lanes + (up[k] + down[k])))
        moved.append(tiles)
    new_p, new_s, new_m = [], [], []
    for k in range(4):
        square = u[k] * u[k] + v[k] * v[k]
        root = square * lax.rsqrt(jnp.maximum(square, SMALLEST))
        drag = (0.02 * ratio / half**2) * root
        new_p.append(wet[k] * (moved[1][k] - (h[k] * slope_e[k] + drag * u[k])))
        new_s.append(wet[k] * (moved[2][k] - (h[k] * slope_n[k] + drag * v[k])))
        settled = (0.3 * ratio / half) * (m[k] * inverse[k])
        new_m.append(moved[3][k] + ((0.05 * ratio / half**2) * square - settled))
    return [moved[0], new_p, new_s, new_m]


def scaled(slopes, ratio):
    slope_e, slope_n, wet = slopes
    return [ratio * a for a in slope_e], [ratio * a for a in slope_n], wet


def flat(nested):
    return jax.tree.leaves(nested)


def combine(function, a, b):
    return jax.tree.map(function, a, b)


def read_tiles(ref, *lead):
    return [[ref[(*lead, field, k)] for k in range(4)] for field in range(FIELDS)]


def write_tiles(ref, state, *lead):
    for field in range(FIELDS):
        for k in range(4):
            ref[(*lead, field, k)] = state[field][k]


def lane_index():
    return lax.broadcasted_iota(jnp.int32, TILE, 1)


def pack_kernel(start_ref, guess_ref, mask_ref, class_ref, table_ref, out_ref):
    time_index = lax.axis_index("tm")
    lanes = lane_index()
    use_start = time_index >= lax.axis_size("tm") - 2
    odd = time_index % 2 == 1

    def windows(plane, chunks):
        ahead = [pltpu.roll(a, 32, 1) for a in chunks]
        behind = [pltpu.roll(a, 96, 1) for a in chunks]
        for c in range(4):
            out_ref[2 * c, plane] = jnp.where(lanes < 32, ahead[c - 1], ahead[c])
            out_ref[2 * c + 1, plane] = jnp.where(lanes < 96, behind[c], behind[(c + 1) % 4])

    cuts = [pl.ds(128 * c, 128) for c in range(4)]
    for field in range(FIELDS):
        windows(
            field,
            [jnp.where(use_start, start_ref[field, :, cut], guess_ref[0, field, :, cut]) for cut in cuts],
        )
    static = []
    for cut in cuts:
        classes = class_ref[:, cut]
        bed = jnp.zeros(TILE, jnp.float32)
        for index in range(table_ref.shape[0]):
            bed = jnp.where(classes == index, table_ref[index], bed)
        static.append(jnp.where(odd, mask_ref[:, cut].astype(jnp.float32), bed))
    windows(FIELDS, static)


SLOTS = {5: 11, 7: 8}
DIVIDE = {5: 205, 7: 147}


def payload(states, width):
    return 8 * states - (-16 * states // SLOTS[width])


def slot_of_lane(width):
    lanes = lane_index()
    right = ((lanes - 64) * DIVIDE[width]) >> 10
    left = (lanes * DIVIDE[width]) >> 10
    inside = jnp.where(lanes < 64, left + 1, right)
    return jnp.where(lanes >= 128 - width, 0, inside)


def fold(ref, states, width):
    lanes, slots = lane_index(), slot_of_lane(width)
    edges = [None] * (payload(len(states), width) - 8 * len(states))
    for index, state in enumerate(states):
        for k in range(4):
            for half in range(2):
                low = pltpu.roll(state[2 * half][k], 96, 1)
                high = pltpu.roll(state[2 * half + 1][k], 32, 1)
                ref[8 * index + 4 * half + k] = jnp.where(lanes < 64, low, high)
                for part, turned in enumerate((low, high)):
                    number = 16 * index + 4 * (2 * half + part) + k
                    edge, slot = divmod(number, SLOTS[width])
                    shift = (64 * part + width * slot) % 128
                    moved = pltpu.roll(turned, shift, 1) if shift else turned
                    edges[edge] = (
                        moved
                        if edges[edge] is None
                        else jnp.where(slots == slot, moved, edges[edge])
                    )
    for index, edge in enumerate(edges):
        ref[8 * len(states) + index] = edge


def unfold(ref, states, width, index=0):
    lanes = lane_index()
    own_lanes = (lanes >= 32) & (lanes < 96)
    state = [[None] * 4 for _ in range(FIELDS)]
    for field in range(FIELDS):
        for k in range(4):
            main = ref[8 * index + 4 * (field // 2) + k]
            own = pltpu.roll(main, 32 if field % 2 == 0 else 96, 1)
            edge, slot = divmod(16 * index + 4 * field + k, SLOTS[width])
            edge = ref[8 * states + edge]
            shift = (32 - width * slot) % 128
            state[field][k] = jnp.where(own_lanes, own, pltpu.roll(edge, shift, 1))
    return state


def forcing_kernel(in_ref, forcing_ref, chain_ref, pass_ref, slope_ref, rows_ref):
    group = lax.axis_index("tm") // 2
    last = group == lax.axis_size("tm") // 2 - 1
    for pair in range(2):
        for r in range(4):
            for plane in range(FIELDS + 1):
                rows_ref[pair, plane, pl.ds(8 * r, 8), :] = in_ref[4 * pair + r, plane]

    def strided(pair, plane):
        return [rows_ref[pair, plane, pl.ds(k, 8, 4), :] for k in range(4)]

    bed, wet = strided(0, FIELDS), strided(1, FIELDS)
    slope_e = [0.5 * (east(a) - west(a)) for a in bed]
    slope_n = [0.5 * (a - b) for a, b in zip(north(bed), south(bed))]
    slopes = (slope_e, slope_n, wet)
    for index, tiles in enumerate(slopes):
        for k in range(4):
            slope_ref[index, k] = tiles[k]
    fine, coarse = scaled(slopes, FINE[0]), scaled(slopes, COARSE[0])
    first = [[strided(pair, field) for field in range(FIELDS)] for pair in range(2)]
    shape = jax.tree.structure(first)

    def propagate(states):
        def body(_, leaves):
            pairs = jax.tree.unflatten(shape, leaves)
            return tuple(flat([advance(state, fine, *FINE) for state in pairs]))

        return jax.tree.unflatten(shape, lax.fori_loop(0, FINE_STEPS, body, tuple(flat(states)), unroll=8))

    def choose(a, b):
        return combine(lambda x, y: jnp.where(last, x, y), a, b)

    before = propagate(first)
    before[0] = choose(first[0], before[0])
    reached = propagate(before)
    forcing = [
        combine(jnp.subtract, reached[pair], advance(before[pair], coarse, *COARSE))
        for pair in range(2)
    ]
    second = combine(jnp.add, advance(reached[0], coarse, *COARSE), forcing[1])
    fold(chain_ref, [second], 7)
    fold(pass_ref, [choose(reached[0], forcing[0]), choose(second, forcing[1])], 5)
    for pair in range(2):
        write_tiles(forcing_ref, forcing[pair], pair)


def coarse_of(slope_ref):
    return scaled([[slope_ref[index, k] for k in range(4)] for index in range(3)], COARSE[0])


def relax(opening, forcing, coarse):
    return combine(jnp.add, advance(opening, coarse, *COARSE), forcing)


def last_kernel(
    far_ref, far_across_ref, middle_ref, middle_across_ref, near_ref, near_across_ref, forcing_ref,
    slope_ref, out_ref, far_join_ref, middle_join_ref, near_join_ref, rows_ref,
):
    starts = lax.axis_index("tm") % RING < 2
    early = starts | (lax.axis_index("tm") % RING >= RING - 4)
    for tile in range(far_ref.shape[0]):
        far_join_ref[tile] = jnp.where(early, far_across_ref[tile], far_ref[tile])
    for tile in range(middle_ref.shape[0]):
        middle_join_ref[tile] = jnp.where(starts, middle_across_ref[tile], middle_ref[tile])
        near_join_ref[tile] = jnp.where(starts, near_across_ref[tile], near_ref[tile])
    lanes = lane_index()
    opens = lax.axis_index("tm") < 2
    coarse = coarse_of(slope_ref)
    value = unfold(far_join_ref, 1, 7)
    for pair in range(2):
        value = relax(value, unfold(middle_join_ref, 2, 5, pair), coarse)
    for position in range(4):
        if position < 2:
            given = unfold(near_join_ref, 2, 5, position)
            value = combine(
                lambda a, b: jnp.where(opens, a, b), given, relax(value, given, coarse)
            )
        else:
            value = relax(value, read_tiles(forcing_ref, position - 2), coarse)
        for field in range(FIELDS):
            shift = 96 if field % 2 == 0 else 32
            for k in range(4):
                rows_ref[position, field, pl.ds(k, 8, 4), :] = pltpu.roll(value[field][k], shift, 1)
        for r in range(4):
            for half in range(2):
                low = rows_ref[position, 2 * half, pl.ds(8 * r, 8), :]
                high = rows_ref[position, 2 * half + 1, pl.ds(8 * r, 8), :]
                out_ref[4 * position + r, half] = jnp.where(lanes < 64, low, high)


def unpack_kernel(in_ref, out_ref):
    lanes = lane_index()
    for half in range(2):
        for c in range(4):
            left, right = in_ref[2 * c, half], in_ref[2 * c + 1, half]
            cut = pl.ds(128 * c, 128)
            out_ref[0, 2 * half, :, cut] = jnp.where(lanes < 64, left, pltpu.roll(right, 64, 1))
            out_ref[0, 2 * half + 1, :, cut] = jnp.where(lanes < 64, pltpu.roll(left, 64, 1), right)


def call(kernel, shapes, specs=None, scratch=(), in_vmem=True, out_vmem=True):
    kind = pltpu.VMEM if out_vmem else jax.ShapeDtypeStruct
    outs = [kind(shape, jnp.float32) for shape in shapes]
    vmem = pl.BlockSpec(memory_space=pltpu.VMEM)
    single = len(outs) == 1

    def run(*args):
        if in_vmem:
            args = [pltpu.with_memory_space_constraint(a, pltpu.VMEM) for a in args]
        return pl.pallas_call(
            kernel,
            out_shape=outs[0] if single else outs,
            in_specs=specs or [vmem] * len(args),
            out_specs=vmem if single else [vmem] * len(outs),
            scratch_shapes=scratch,
        )(*args)

    return run


def groups(count, row_devices, size):
    return [
        [(size * g + q) * row_devices + r for q in range(size) for r in range(row_devices)]
        for g in range(count // size)
    ]


def on_device(start_state, initial_guess, land_mask, bed_class, bed_table):
    count, row_devices = lax.axis_size("tm"), lax.axis_size("rows")
    vmem = pl.BlockSpec(memory_space=pltpu.VMEM)
    smem = pl.BlockSpec(memory_space=pltpu.SMEM)
    packed = call(
        pack_kernel, [(8, FIELDS + 1, *TILE)], [vmem] * 4 + [smem], in_vmem=False
    )(start_state, initial_guess, land_mask, bed_class, bed_table)
    arrived = lax.all_to_all(packed, AXES, 0, 0, axis_index_groups=groups(count, row_devices, 2))
    state = (FIELDS, 4, *TILE)
    forcing, chain, passed, slopes = call(
        forcing_kernel,
        [(2, *state), (payload(1, 7), *TILE), (payload(2, 5), *TILE), (3, 4, *TILE)],
        scratch=[pltpu.VMEM((2, FIELDS + 1, 32, 128), jnp.float32)],
    )(arrived)
    even = [i for i in range(count) if i % 4 < 2]
    odd = [i for i in range(count) if i % 4 >= 2]
    two = [(i, (i + 2) % count) for i in odd]
    four = [(i, i + 4) for i in even if i + 4 < count]
    six = [(i, (i + 6) % count) for i in odd if i < count - 6 or i >= count - 2]

    def send(value, pairs):
        return lax.ppermute(value, "tm", pairs)

    far_across = send(chain, [(i, j) for i, j in six if j % RING < 2 or j % RING >= RING - 4])
    middle_across = send(passed, [(i, j) for i, j in four if j % RING < 2])
    near_across = send(passed, [(i, j) for i, j in two if j % RING < 2])
    near = send(passed, [(i, j) for i, j in two if j % RING >= 2])
    far = send(chain, [(i, j) for i, j in six if 2 <= j % RING < RING - 4])
    middle = send(passed, [(i, j) for i, j in four if j % RING >= 2])
    packed = call(
        last_kernel,
        [(16, 2, *TILE)],
        scratch=[
            pltpu.VMEM((payload(1, 7), *TILE), jnp.float32),
            pltpu.VMEM((payload(2, 5), *TILE), jnp.float32),
            pltpu.VMEM((payload(2, 5), *TILE), jnp.float32),
            pltpu.VMEM((4, FIELDS, 32, 128), jnp.float32),
        ],
    )(far, far_across, middle, middle_across, near, near_across, forcing, slopes)
    arrived = lax.all_to_all(packed, AXES, 0, 0, axis_index_groups=groups(count, row_devices, 4))
    return call(unpack_kernel, [initial_guess.shape], out_vmem=False)(arrived)


def solution(mesh):
    in_specs = (
        P(None, "rows", None),
        P("tm", None, "rows", None),
        P("rows", None),
        P("rows", None),
        P(),
    )
    out_specs = P("tm", None, "rows", None)
    return jax.shard_map(
        on_device, mesh=mesh, in_specs=in_specs, out_specs=out_specs, check_vma=False
    )
```

```python
import jax
import jax.numpy as jnp
from jax import lax
from jax.experimental import pallas as pl
from jax.experimental.pallas import tpu as pltpu
from jax.sharding import PartitionSpec as P


FINE_STEPS = 8
FINE = (0.0375, 0.025)
COARSE = (0.3, 0.2)
FIELDS = 4
TILE = (8, 128)
AXES = ("tm", "rows")
SMALLEST = 1.1754944e-38
RING = 16


def east(x):
    return pltpu.roll(x, 127, 1)


def west(x):
    return pltpu.roll(x, 1, 1)


def north(tiles):
    return [*tiles[1:], pltpu.roll(tiles[0], 7, 0)]


def south(tiles):
    return [pltpu.roll(tiles[3], 1, 0), *tiles[:3]]


def advance(state, statics, ratio, viscous):
    slope_e, slope_n, wet = statics
    half = 0.5 * ratio
    h, p, s, m = state
    inverse = [half / a for a in h]
    u = [a * b for a, b in zip(p, inverse)]
    v = [a * b for a, b in zip(s, inverse)]
    pressure = [(0.5 * half) * (a * a) for a in h]
    cross = [a * b for a, b in zip(s, u)]
    east_flux = (
        [half * a for a in p],
        [a * b + c for a, b, c in zip(p, u, pressure)],
        cross,
        [a * b for a, b in zip(m, u)],
    )
    north_flux = (
        [half * a for a in s],
        cross,
        [a * b + c for a, b, c in zip(s, v, pressure)],
        [a * b for a, b in zip(m, v)],
    )
    moved = []
    for field in range(FIELDS):
        q = state[field]
        near = [viscous * a for a in q]
        up = north([a - b for a, b in zip(near, north_flux[field])])
        down = south([a + b for a, b in zip(near, north_flux[field])])
        tiles = []
        for k in range(4):
            lanes = east(near[k] - east_flux[field][k]) + west(near[k] + east_flux[field][k])
            tiles.append((1.0 - 4.0 * viscous) * q[k] + (lanes + (up[k] + down[k])))
        moved.append(tiles)
    new_p, new_s, new_m = [], [], []
    for k in range(4):
        square = u[k] * u[k] + v[k] * v[k]
        root = square * lax.rsqrt(jnp.maximum(square, SMALLEST))
        drag = (0.02 * ratio / half**2) * root
        new_p.append(wet[k] * (moved[1][k] - (h[k] * slope_e[k] + drag * u[k])))
        new_s.append(wet[k] * (moved[2][k] - (h[k] * slope_n[k] + drag * v[k])))
        settled = (0.3 * ratio / half) * (m[k] * inverse[k])
        new_m.append(moved[3][k] + ((0.05 * ratio / half**2) * square - settled))
    return [moved[0], new_p, new_s, new_m]


def scaled(slopes, ratio):
    slope_e, slope_n, wet = slopes
    return [ratio * a for a in slope_e], [ratio * a for a in slope_n], wet


def flat(nested):
    return jax.tree.leaves(nested)


def combine(function, a, b):
    return jax.tree.map(function, a, b)


def read_tiles(ref, *lead):
    return [[ref[(*lead, field, k)] for k in range(4)] for field in range(FIELDS)]


def write_tiles(ref, state, *lead):
    for field in range(FIELDS):
        for k in range(4):
            ref[(*lead, field, k)] = state[field][k]


def lane_index():
    return lax.broadcasted_iota(jnp.int32, TILE, 1)


def pack_kernel(start_ref, guess_ref, mask_ref, class_ref, table_ref, out_ref):
    time_index = lax.axis_index("tm")
    lanes = lane_index()
    use_start = time_index >= lax.axis_size("tm") - 2
    odd = time_index % 2 == 1

    def windows(plane, chunks):
        ahead = [pltpu.roll(a, 32, 1) for a in chunks]
        behind = [pltpu.roll(a, 96, 1) for a in chunks]
        for c in range(4):
            out_ref[2 * c, plane] = jnp.where(lanes < 32, ahead[c - 1], ahead[c])
            out_ref[2 * c + 1, plane] = jnp.where(lanes < 96, behind[c], behind[(c + 1) % 4])

    cuts = [pl.ds(128 * c, 128) for c in range(4)]
    for field in range(FIELDS):
        windows(
            field,
            [jnp.where(use_start, start_ref[field, :, cut], guess_ref[0, field, :, cut]) for cut in cuts],
        )
    static = []
    for cut in cuts:
        classes = class_ref[:, cut]
        bed = jnp.zeros(TILE, jnp.float32)
        for index in range(table_ref.shape[0]):
            bed = jnp.where(classes == index, table_ref[index], bed)
        static.append(jnp.where(odd, mask_ref[:, cut].astype(jnp.float32), bed))
    windows(FIELDS, static)


SLOTS = {5: 11, 7: 8}
DIVIDE = {5: 205, 7: 147}


def payload(states, width):
    return 8 * states - (-16 * states // SLOTS[width])


def slot_of_lane(width):
    lanes = lane_index()
    right = ((lanes - 64) * DIVIDE[width]) >> 10
    left = (lanes * DIVIDE[width]) >> 10
    inside = jnp.where(lanes < 64, left + 1, right)
    return jnp.where(lanes >= 128 - width, 0, inside)


def fold(ref, states, width):
    lanes, slots = lane_index(), slot_of_lane(width)
    edges = [None] * (payload(len(states), width) - 8 * len(states))
    for index, state in enumerate(states):
        for k in range(4):
            for half in range(2):
                low = pltpu.roll(state[2 * half][k], 96, 1)
                high = pltpu.roll(state[2 * half + 1][k], 32, 1)
                ref[8 * index + 4 * half + k] = jnp.where(lanes < 64, low, high)
                for part, turned in enumerate((low, high)):
                    number = 16 * index + 4 * (2 * half + part) + k
                    edge, slot = divmod(number, SLOTS[width])
                    shift = (64 * part + width * slot) % 128
                    moved = pltpu.roll(turned, shift, 1) if shift else turned
                    edges[edge] = (
                        moved
                        if edges[edge] is None
                        else jnp.where(slots == slot, moved, edges[edge])
                    )
    for index, edge in enumerate(edges):
        ref[8 * len(states) + index] = edge


def unfold(ref, states, width, index=0):
    lanes = lane_index()
    own_lanes = (lanes >= 32) & (lanes < 96)
    state = [[None] * 4 for _ in range(FIELDS)]
    for field in range(FIELDS):
        for k in range(4):
            main = ref[8 * index + 4 * (field // 2) + k]
            own = pltpu.roll(main, 32 if field % 2 == 0 else 96, 1)
            edge, slot = divmod(16 * index + 4 * field + k, SLOTS[width])
            edge = ref[8 * states + edge]
            shift = (32 - width * slot) % 128
            state[field][k] = jnp.where(own_lanes, own, pltpu.roll(edge, shift, 1))
    return state


def forcing_kernel(in_ref, forcing_ref, chain_ref, pass_ref, slope_ref, rows_ref):
    group = lax.axis_index("tm") // 2
    last = group == lax.axis_size("tm") // 2 - 1
    for pair in range(2):
        for r in range(4):
            for plane in range(FIELDS + 1):
                rows_ref[pair, plane, pl.ds(8 * r, 8), :] = in_ref[4 * pair + r, plane]

    def strided(pair, plane):
        return [rows_ref[pair, plane, pl.ds(k, 8, 4), :] for k in range(4)]

    bed, wet = strided(0, FIELDS), strided(1, FIELDS)
    slope_e = [0.5 * (east(a) - west(a)) for a in bed]
    slope_n = [0.5 * (a - b) for a, b in zip(north(bed), south(bed))]
    slopes = (slope_e, slope_n, wet)
    for index, tiles in enumerate(slopes):
        for k in range(4):
            slope_ref[index, k] = tiles[k]
    fine, coarse = scaled(slopes, FINE[0]), scaled(slopes, COARSE[0])
    first = [[strided(pair, field) for field in range(FIELDS)] for pair in range(2)]
    shape = jax.tree.structure(first)

    def propagate(states):
        def body(_, leaves):
            pairs = jax.tree.unflatten(shape, leaves)
            return tuple(flat([advance(state, fine, *FINE) for state in pairs]))

        return jax.tree.unflatten(shape, lax.fori_loop(0, FINE_STEPS, body, tuple(flat(states)), unroll=8))

    def choose(a, b):
        return combine(lambda x, y: jnp.where(last, x, y), a, b)

    before = propagate(first)
    before[0] = choose(first[0], before[0])
    reached = propagate(before)
    forcing = [
        combine(jnp.subtract, reached[pair], advance(before[pair], coarse, *COARSE))
        for pair in range(2)
    ]
    second = combine(jnp.add, advance(reached[0], coarse, *COARSE), forcing[1])
    fold(chain_ref, [second], 7)
    fold(pass_ref, [choose(reached[0], forcing[0]), choose(second, forcing[1])], 5)
    for pair in range(2):
        write_tiles(forcing_ref, forcing[pair], pair)


def coarse_of(slope_ref):
    return scaled([[slope_ref[index, k] for k in range(4)] for index in range(3)], COARSE[0])


def relax(opening, forcing, coarse):
    return combine(jnp.add, advance(opening, coarse, *COARSE), forcing)


def last_kernel(
    far_ref, far_across_ref, middle_ref, middle_across_ref, near_ref, near_across_ref, forcing_ref,
    slope_ref, out_ref, far_join_ref, middle_join_ref, near_join_ref, rows_ref,
):
    starts = lax.axis_index("tm") % RING < 2
    early = starts
    for tile in range(far_ref.shape[0]):
        far_join_ref[tile] = jnp.where(early, far_across_ref[tile], far_ref[tile])
    for tile in range(middle_ref.shape[0]):
        middle_join_ref[tile] = jnp.where(starts, middle_across_ref[tile], middle_ref[tile])
        near_join_ref[tile] = jnp.where(starts, near_across_ref[tile], near_ref[tile])
    lanes = lane_index()
    opens = lax.axis_index("tm") < 2
    coarse = coarse_of(slope_ref)
    value = unfold(far_join_ref, 1, 7)
    for pair in range(2):
        value = relax(value, unfold(middle_join_ref, 2, 5, pair), coarse)
    for position in range(4):
        if position < 2:
            given = unfold(near_join_ref, 2, 5, position)
            value = combine(
                lambda a, b: jnp.where(opens, a, b), given, relax(value, given, coarse)
            )
        else:
            value = relax(value, read_tiles(forcing_ref, position - 2), coarse)
        for field in range(FIELDS):
            shift = 96 if field % 2 == 0 else 32
            for k in range(4):
                rows_ref[position, field, pl.ds(k, 8, 4), :] = pltpu.roll(value[field][k], shift, 1)
        for r in range(4):
            for half in range(2):
                low = rows_ref[position, 2 * half, pl.ds(8 * r, 8), :]
                high = rows_ref[position, 2 * half + 1, pl.ds(8 * r, 8), :]
                out_ref[4 * position + r, half] = jnp.where(lanes < 64, low, high)


def unpack_kernel(in_ref, out_ref):
    lanes = lane_index()
    for half in range(2):
        for c in range(4):
            left, right = in_ref[2 * c, half], in_ref[2 * c + 1, half]
            cut = pl.ds(128 * c, 128)
            out_ref[0, 2 * half, :, cut] = jnp.where(lanes < 64, left, pltpu.roll(right, 64, 1))
            out_ref[0, 2 * half + 1, :, cut] = jnp.where(lanes < 64, pltpu.roll(left, 64, 1), right)


def call(kernel, shapes, specs=None, scratch=(), in_vmem=True, out_vmem=True):
    kind = pltpu.VMEM if out_vmem else jax.ShapeDtypeStruct
    outs = [kind(shape, jnp.float32) for shape in shapes]
    vmem = pl.BlockSpec(memory_space=pltpu.VMEM)
    single = len(outs) == 1

    def run(*args):
        if in_vmem:
            args = [pltpu.with_memory_space_constraint(a, pltpu.VMEM) for a in args]
        return pl.pallas_call(
            kernel,
            out_shape=outs[0] if single else outs,
            in_specs=specs or [vmem] * len(args),
            out_specs=vmem if single else [vmem] * len(outs),
            scratch_shapes=scratch,
        )(*args)

    return run


def groups(count, row_devices, size):
    return [
        [(size * g + q) * row_devices + r for q in range(size) for r in range(row_devices)]
        for g in range(count // size)
    ]


def on_device(start_state, initial_guess, land_mask, bed_class, bed_table):
    count, row_devices = lax.axis_size("tm"), lax.axis_size("rows")
    vmem = pl.BlockSpec(memory_space=pltpu.VMEM)
    smem = pl.BlockSpec(memory_space=pltpu.SMEM)
    packed = call(
        pack_kernel, [(8, FIELDS + 1, *TILE)], [vmem] * 4 + [smem], in_vmem=False
    )(start_state, initial_guess, land_mask, bed_class, bed_table)
    arrived = lax.all_to_all(packed, AXES, 0, 0, axis_index_groups=groups(count, row_devices, 2))
    state = (FIELDS, 4, *TILE)
    forcing, chain, passed, slopes = call(
        forcing_kernel,
        [(2, *state), (payload(1, 7), *TILE), (payload(2, 5), *TILE), (3, 4, *TILE)],
        scratch=[pltpu.VMEM((2, FIELDS + 1, 32, 128), jnp.float32)],
    )(arrived)
    even = [i for i in range(count) if i % 4 < 2]
    odd = [i for i in range(count) if i % 4 >= 2]
    two = [(i, (i + 2) % count) for i in odd]
    four = [(i, i + 4) for i in even if i + 4 < count]
    six = [(i, (i + 6) % count) for i in odd if i < count - 6 or i >= count - 2]

    def send(value, pairs):
        return lax.ppermute(value, "tm", pairs)

    far_across = send(chain, [(i, j) for i, j in six if j % RING < 2])
    middle_across = send(passed, [(i, j) for i, j in four if j % RING < 2])
    near_across = send(passed, [(i, j) for i, j in two if j % RING < 2])
    near = send(passed, [(i, j) for i, j in two if j % RING >= 2])
    far = send(chain, [(i, j) for i, j in six if j % RING >= 2])
    middle = send(passed, [(i, j) for i, j in four if j % RING >= 2])
    packed = call(
        last_kernel,
        [(16, 2, *TILE)],
        scratch=[
            pltpu.VMEM((payload(1, 7), *TILE), jnp.float32),
            pltpu.VMEM((payload(2, 5), *TILE), jnp.float32),
            pltpu.VMEM((payload(2, 5), *TILE), jnp.float32),
            pltpu.VMEM((4, FIELDS, 32, 128), jnp.float32),
        ],
    )(far, far_across, middle, middle_across, near, near_across, forcing, slopes)
    arrived = lax.all_to_all(packed, AXES, 0, 0, axis_index_groups=groups(count, row_devices, 4))
    return call(unpack_kernel, [initial_guess.shape], out_vmem=False)(arrived)


def solution(mesh):
    in_specs = (
        P(None, "rows", None),
        P("tm", None, "rows", None),
        P("rows", None),
        P("rows", None),
        P(),
    )
    out_specs = P("tm", None, "rows", None)
    return jax.shard_map(
        on_device, mesh=mesh, in_specs=in_specs, out_specs=out_specs, check_vma=False
    )
```
